256 devices in a mesh: group: 16 (over x, y_hi, core), member: 16 (over y_lo, z).
Axes of the slice: x: 4, y: 4 (y_hi: 2, y_lo: 2; y = y_hi * 2 + y_lo), z: 8, core: 2. Of those that a mesh axis runs over, the one named last changes fastest.
Arguments:
- spectra: bfloat16 [8192, 8, 2048], P(('group', 'member'))
- partner: int32 [16], replicated, may hold values from 0 to 15, as said below
Outputs:
- correlations: bfloat16 [8192, 512, 128], P(('group', 'member'))
The draws below stay inside these ranges and needn't reach their ends.
Inputs may be any that keep to these rules, and one draw needn't show every extreme that they name: partner is one round of a round-robin among the 16 groups: partner[partner[g]] == g and partner[g] != g for every g.
All inputs are finite; a program needn't handle non-finite values.
Results may differ from the reference program's by a relative error of at most 0.007.
Values may be sent and summed in bfloat16 or wider, within the bound.
A program may use at most 192 MiB of HBM per device.

```python
import math
import jax
import jax.numpy as jnp
from jax import lax

CH_DEV = 32
WINDOWS = 8
FREQS = 1024
LAGS = 128
HALF = 64
GROUP_CH = 512
CHANNELS = 8192
N_GROUP = 16
N_MEMBER = 16


def draw_spectra(key, part):
    keys = jax.random.split(key, 6)
    positions = jnp.arange(FREQS).astype(jnp.float32)
    spread_top = math.log(10.0)
    channel_gain = jnp.exp(jax.random.uniform(keys[0], (CHANNELS, 1, 1), jnp.float32, 0.0, spread_top))
    window_gain = jnp.exp(jax.random.uniform(keys[1], (CHANNELS, WINDOWS, 1), jnp.float32, 0.0, math.log(3.0)))
    tilt = jax.random.uniform(keys[2], (CHANNELS, 1, 1), jnp.float32, 1.0, 4.0)
    phase = jax.random.uniform(keys[3], (CHANNELS, 1, 1), jnp.float32, 0.0, 2.0 * math.pi)
    shape_gain = jnp.exp(0.5 * math.log(10.0) * (1.0 + jnp.sin(2.0 * math.pi * tilt * positions / FREQS + phase)))
    rough = jax.random.uniform(keys[4], (CHANNELS, WINDOWS, FREQS), jnp.float32, 0.5, 1.5)
    amplitude = channel_gain * window_gain * shape_gain * rough
    noise = jax.random.normal(keys[5], (CHANNELS, WINDOWS, 2, FREQS), jnp.float32)
    values = noise * amplitude[:, :, None, :]
    return values.reshape(CHANNELS, WINDOWS, 2 * FREQS).astype(jnp.bfloat16)


def draw_partner(key, part):
    round_key = jax.random.fold_in(key, 11)
    label_key = jax.random.fold_in(key, 23)
    group_count = N_GROUP
    odd_count = group_count - 1
    round_index = jax.random.randint(round_key, (), 0, odd_count, dtype=jnp.int32)
    positions = jnp.arange(group_count, dtype=jnp.int32)
    paired = jnp.mod(round_index - positions, odd_count)
    paired = jnp.where(paired == positions, odd_count, paired)
    last_pair = jnp.mod(round_index * (group_count // 2), odd_count)
    base = jnp.where(positions == odd_count, last_pair, paired).astype(jnp.int32)
    labels = jax.random.permutation(label_key, group_count).astype(jnp.int32)
    inverse = jnp.argsort(labels, stable=True).astype(jnp.int32)
    return labels[base[inverse]].astype(jnp.int32)


def setup_inputs(seed: int = 0) -> dict:
    key_of = jax.random.split(jax.random.key(seed), 3)
    spectra = draw_spectra(jax.random.fold_in(key_of[2], 71), 0)
    partner = draw_partner(jax.random.fold_in(key_of[2], 71), 0)
    return {"spectra": spectra, "partner": partner}


def band_matrix(freq_count):
    positions = jnp.arange(freq_count, dtype=jnp.int32)
    distance = jnp.abs(positions[:, None] - positions[None, :])
    band_ones = (distance <= HALF).astype(jnp.float32)
    counts = (jnp.minimum(positions + HALF, freq_count - 1) - jnp.maximum(positions - HALF, 0) + 1).astype(jnp.float32)
    return (band_ones, counts)

def whiten(spectra):
    freq_count = spectra.shape[2] // 2
    window_count = spectra.shape[1]
    real_part = spectra[:, :, :freq_count].astype(jnp.float32)
    imag_part = spectra[:, :, freq_count:].astype(jnp.float32)
    power_sum = lax.optimization_barrier(jnp.sum(real_part * real_part + imag_part * imag_part, axis=1))
    band_ones, counts = band_matrix(freq_count)
    smoothed = jnp.dot(power_sum, band_ones, precision=lax.Precision.HIGHEST)
    average = smoothed / (counts * window_count)
    inverse_amp = 1.0 / jnp.sqrt(average + 1e-05)
    factor = jnp.concatenate([inverse_amp, inverse_amp], axis=1)
    return (spectra.astype(jnp.float32) * factor[:, None, :]).astype(jnp.bfloat16)

def lag_matrix(freq_count, window_count):
    lag_values = jnp.arange(LAGS, dtype=jnp.int32) - LAGS // 2
    freq_values = jnp.arange(freq_count, dtype=jnp.int32)
    residue = jnp.mod(freq_values[:, None] * lag_values[None, :], 2 * freq_count)
    angles = jnp.pi * residue.astype(jnp.float32) / freq_count
    norm_factor = 1.0 / math.sqrt(window_count * freq_count)
    return jnp.concatenate([jnp.cos(angles) * norm_factor, -jnp.sin(angles) * norm_factor], axis=0).astype(jnp.bfloat16)

def correlate(own_rows, other_rows, lag_table):
    freq_count = own_rows.shape[2] // 2
    own_real = own_rows[:, :, :freq_count].astype(jnp.float32)
    own_imag = own_rows[:, :, freq_count:].astype(jnp.float32)
    other_real = other_rows[:, :, :freq_count].astype(jnp.float32)
    other_imag = other_rows[:, :, freq_count:].astype(jnp.float32)
    left_real = jnp.concatenate([own_real, own_imag], axis=1)
    left_imag = jnp.concatenate([own_imag, -own_real], axis=1)
    right_part = jnp.concatenate([other_real, other_imag], axis=1)
    cross_real = jnp.einsum('awf,bwf->abf', left_real, right_part, precision=lax.Precision.HIGHEST)
    cross_imag = jnp.einsum('awf,bwf->abf', left_imag, right_part, precision=lax.Precision.HIGHEST)
    cross = jnp.concatenate([cross_real, cross_imag], axis=2).astype(jnp.bfloat16)
    own_count = own_rows.shape[0]
    other_count = other_rows.shape[0]
    lagged = jnp.dot(cross.reshape(own_count * other_count, 2 * freq_count), lag_table, preferred_element_type=jnp.float32)
    return lagged.reshape(own_count, other_count, lag_table.shape[1])

def reference(spectra, partner):
    whitened = whiten(spectra)
    lag_table = lag_matrix(FREQS, WINDOWS)
    block_total = CHANNELS // CH_DEV

    def one_block(block_index):
        group_index = block_index // N_MEMBER
        partner_group = partner[group_index]
        own_rows = lax.dynamic_slice_in_dim(whitened, (block_index * CH_DEV).astype(jnp.int32), CH_DEV, 0)
        other_rows = lax.dynamic_slice_in_dim(whitened, (partner_group * GROUP_CH).astype(jnp.int32), GROUP_CH, 0)
        return correlate(own_rows, other_rows, lag_table).astype(jnp.bfloat16)
    stacked = lax.map(one_block, jnp.arange(block_total, dtype=jnp.int32))
    return stacked.reshape(CHANNELS, GROUP_CH, LAGS)
```

```python
import functools
import math

import jax
import jax.numpy as jnp
from jax import lax
from jax.experimental import pallas as pl
from jax.experimental.pallas import tpu as pltpu
from jax.sharding import Mesh
from jax.sharding import PartitionSpec as P

LAGS = 128
HALF = 64
FREQS = 1024
WINDOWS = 8
CH = 32
COLS = 128
INNER = 8
CHUNK = 16
STEPS = COLS // CHUNK
TILE = 256
AXES = ("x", "yh", "core", "ylo", "z")
MESH = pl.DeviceIdType.MESH

SLOT = {0: 0, 1: 1, -1: 2, 2: 3, -2: 4, 3: 5, -3: 6, 4: 7}
DIST = {slot: dist for dist, slot in SLOT.items()}


def band_matrix():
    positions = jnp.arange(FREQS, dtype=jnp.int32)
    distance = jnp.abs(positions[:, None] - positions[None, :])
    band_ones = (distance <= HALF).astype(jnp.float32)
    counts = (
        jnp.minimum(positions + HALF, FREQS - 1) - jnp.maximum(positions - HALF, 0) + 1
    ).astype(jnp.float32)
    return band_ones, counts


def whiten(spectra):
    real_part = spectra[:, :, :FREQS].astype(jnp.float32)
    imag_part = spectra[:, :, FREQS:].astype(jnp.float32)
    power_sum = jnp.sum(real_part * real_part + imag_part * imag_part, axis=1)
    band_ones, counts = band_matrix()
    smoothed = jnp.dot(power_sum, band_ones, precision=lax.Precision.HIGHEST)
    average = smoothed / (counts * WINDOWS)
    inverse_amp = 1.0 / jnp.sqrt(average + 1e-05)
    factor = jnp.concatenate([inverse_amp, inverse_amp], axis=1)
    return (spectra.astype(jnp.float32) * factor[:, None, :]).astype(jnp.bfloat16)


def lag_rows():
    lag_values = jnp.arange(LAGS, dtype=jnp.int32) - LAGS // 2
    columns = jnp.arange(COLS, dtype=jnp.int32).reshape(STEPS, CHUNK)
    freq = columns[:, :, None] + COLS * jnp.arange(INNER, dtype=jnp.int32)[None, None, :]
    residue = jnp.mod(freq[:, None, :, :] * lag_values[None, :, None, None], 2 * FREQS)
    angles = jnp.pi * residue.astype(jnp.float32) / FREQS
    norm_factor = 1.0 / math.sqrt(WINDOWS * FREQS)
    table = jnp.stack([jnp.cos(angles) * norm_factor, -jnp.sin(angles) * norm_factor], axis=3)
    return table.reshape(STEPS, LAGS, CHUNK * 2 * INNER).astype(jnp.bfloat16)


def pair_kernel(
    own_ref, part_ref, lag_ref, out_ref,
    x_rows, xs_rows, gathered, left, cross, total, result,
    own_sem, recv_sem, send_sem, out_send, out_recv,
):
    core = lax.axis_index("core")
    ylo = lax.axis_index("ylo")
    z = lax.axis_index("z")
    up = lax.rem(z + 1, 8)
    down = lax.rem(z + 7, 8)
    moved = core != ylo

    barrier = pltpu.get_barrier_semaphore()
    pl.semaphore_signal(barrier, inc=1, device_id={"z": up}, device_id_type=MESH)
    pl.semaphore_signal(barrier, inc=1, device_id={"z": down}, device_id_type=MESH)
    pl.semaphore_signal(barrier, inc=1, device_id={"core": 1 - core}, device_id_type=MESH)

    @pl.when(moved)
    def _():
        pl.semaphore_signal(
            barrier, inc=1, device_id={"core": ylo, "ylo": core}, device_id_type=MESH
        )
        pl.semaphore_wait(barrier, 4)

    @pl.when(jnp.logical_not(moved))
    def _():
        pl.semaphore_wait(barrier, 3)

    def columns(c):
        return pl.ds(pl.multiple_of(c * CHUNK, CHUNK), CHUNK)

    def place(c, dist, member):
        start = SLOT[dist] * 64 + member * 32
        return gathered.at[columns(c), pl.ds(pl.multiple_of(start, 32), 32), :]

    def source(c, dist):
        return part_ref.at[columns(c)] if dist == 0 else place(c, dist, core)

    def hop(c, dist, step):
        landed = 4 if dist + step == -4 else dist + step
        return pltpu.make_async_remote_copy(
            src_ref=source(c, dist),
            dst_ref=place(c, landed, core),
            send_sem=send_sem.at[c, SLOT[landed] - 1],
            recv_sem=recv_sem.at[c, 0, SLOT[landed]],
            device_id={"z": down if step == 1 else up},
            device_id_type=MESH,
        )

    def across(c, dist):
        return pltpu.make_async_remote_copy(
            src_ref=source(c, dist),
            dst_ref=place(c, dist, core),
            send_sem=send_sem.at[c, 7 + SLOT[dist]],
            recv_sem=recv_sem.at[c, 1, SLOT[dist]],
            device_id={"core": 1 - core},
            device_id_type=MESH,
        )

    def own_copy(c):
        return pltpu.make_async_copy(part_ref.at[columns(c)], place(c, 0, core), own_sem.at[c])

    def result_pieces(tile):
        for piece in range(4):
            from_z = lax.rem(z + DIST[tile * 4 + piece] + 8, 8)
            for member in range(2):
                rows = pl.ds(piece * 64 + member * 32, 32)
                target = pl.ds(pl.multiple_of((member * 8 + from_z) * 32, 32), 32)
                yield tile * 8 + piece * 2 + member, result.at[tile, :, rows, :], target

    def result_remote(index, src, target):
        return pltpu.make_async_remote_copy(
            src_ref=src, dst_ref=out_ref.at[:, target, :],
            send_sem=out_send.at[index], recv_sem=out_recv.at[index],
            device_id={"core": ylo, "ylo": core}, device_id_type=MESH,
        )

    def result_local(index, src, target):
        return pltpu.make_async_copy(src, out_ref.at[:, target, :], out_send.at[index])

    def send_result(tile):
        @pl.when(moved)
        def _():
            for piece in result_pieces(tile):
                result_remote(*piece).start()

        @pl.when(jnp.logical_not(moved))
        def _():
            for piece in result_pieces(tile):
                result_local(*piece).start()

    lane = lax.broadcasted_iota(jnp.int32, (INNER, COLS), 1)
    row = lax.broadcasted_iota(jnp.int32, (INNER, COLS), 0)
    mask = lax.rem(lane // WINDOWS, INNER) == row
    sign = jnp.where(lax.broadcasted_iota(jnp.int32, (CH, COLS), 1) < 64, 1.0, -1.0)

    def load_rows(column):
        value = own_ref[column].astype(jnp.float32)
        x_rows[column] = value
        xs_rows[column] = pltpu.roll(value, 64, 1) * sign

    def cross_column(c, i, tile):
        column = c * CHUNK + i
        for a in range(CH):
            re_row = jnp.broadcast_to(x_rows[column, pl.ds(a, 1), :], (INNER, COLS))
            im_row = jnp.broadcast_to(xs_rows[column, pl.ds(a, 1), :], (INNER, COLS))
            block = jnp.concatenate(
                [jnp.where(mask, re_row, 0.0), jnp.where(mask, im_row, 0.0)], axis=0
            )
            left[pl.ds(a * 16, 16), :] = block.astype(jnp.bfloat16)
        right = gathered[column, pl.ds(pl.multiple_of(tile * TILE, TILE), TILE), :]
        product = lax.dot_general(
            left[...], right, (((1,), (1,)), ((), ())), preferred_element_type=jnp.float32
        )
        cross[:, pl.ds(pl.multiple_of(i * 16, 16), 16), :] = product.astype(
            jnp.bfloat16
        ).reshape(CH, 16, TILE)

    def lag_channel(c, a, first):
        product = jnp.dot(lag_ref[c], cross[a], preferred_element_type=jnp.float32)

        @pl.when(first)
        def _():
            total[a] = product

        @pl.when(jnp.logical_not(first))
        def _():
            total[a] = total[a] + product

    def compute(c, tile):
        @pl.loop(0, CHUNK)
        def _(i):
            cross_column(c, i, tile)

        @pl.loop(0, CH)
        def _(a):
            lag_channel(c, a, c == 0)

        @pl.when(c == STEPS - 1)
        def _():
            @pl.loop(0, CH)
            def _(a):
                result[tile, a] = total[a].T.astype(jnp.bfloat16)

    def inside(c):
        return jnp.logical_and(c >= 0, c < STEPS)

    @pl.loop(0, 2 * STEPS + 3)
    def _(tick):
        t = tick - 3

        @pl.when(inside(t + 3))
        def _():
            c = t + 3
            own_copy(c).start()
            hop(c, 0, 1).start()
            hop(c, 0, -1).start()
            across(c, 0).start()

        @pl.when(inside(t + 2))
        def _():
            c = t + 2
            hop(c, 0, 1).wait_recv()
            hop(c, 1, 1).start()
            hop(c, 0, -1).wait_recv()
            hop(c, -1, -1).start()
            across(c, 1).start()
            across(c, -1).start()

        @pl.when(inside(t + 1))
        def _():
            c = t + 1
            hop(c, 1, 1).wait_recv()
            across(c, 2).start()
            hop(c, -1, -1).wait_recv()
            across(c, -2).start()

        @pl.when(inside(t - 5))
        def _():
            c = t - 5
            hop(c, 2, 1).start()
            hop(c, -2, -1).start()

        @pl.when(inside(t - 6))
        def _():
            c = t - 6
            hop(c, 2, 1).wait_recv()
            hop(c, -2, -1).wait_recv()

            @pl.when(lax.rem(c, 2) == 0)
            def _():
                hop(c, 3, 1).start()

            @pl.when(lax.rem(c, 2) == 1)
            def _():
                hop(c, -3, -1).start()

            across(c, 3).start()
            across(c, -3).start()

        @pl.when(inside(t - 7))
        def _():
            c = t - 7
            hop(c, 3, 1).wait_recv()
            across(c, 4).start()

        @pl.when(t < 0)
        def _():
            @pl.loop(0, 43)
            def _(i):
                load_rows(jnp.minimum((t + 3) * 43 + i, COLS - 1))

        @pl.when(inside(t))
        def _():
            own_copy(t).wait()
            for dist in (0, 1, -1, 2):
                across(t, dist).wait_recv()
            compute(t, 0)

        @pl.when(t == STEPS)
        def _():
            send_result(0)

        @pl.when(t >= STEPS)
        def _():
            for dist in (-2, 3, -3, 4):
                across(t - STEPS, dist).wait_recv()
            compute(t - STEPS, 1)

    send_result(1)

    @pl.loop(0, STEPS)
    def _(c):
        for dist, step in ((0, 1), (0, -1), (1, 1), (-1, -1), (2, 1), (-2, -1), (3, 1)):
            hop(c, dist, step).wait_send()
        for dist in DIST.values():
            across(c, dist).wait_send()

    @pl.when(moved)
    def _():
        for tile in range(2):
            for piece in result_pieces(tile):
                result_remote(*piece).wait()

    @pl.when(jnp.logical_not(moved))
    def _():
        for tile in range(2):
            for piece in result_pieces(tile):
                result_local(*piece).wait()


def correlate_pairs(own, part, table):
    return pl.pallas_call(
        pair_kernel,
        out_shape=jax.ShapeDtypeStruct((CH, 16 * CH, LAGS), jnp.bfloat16),
        in_specs=[
            pl.BlockSpec(memory_space=pltpu.VMEM),
            pl.BlockSpec(memory_space=pl.ANY),
            pl.BlockSpec(memory_space=pltpu.VMEM),
        ],
        out_specs=pl.BlockSpec(memory_space=pl.ANY),
        scratch_shapes=[
            pltpu.VMEM((COLS, CH, COLS), jnp.float32),
            pltpu.VMEM((COLS, CH, COLS), jnp.float32),
            pltpu.VMEM((COLS, 16 * CH, COLS), jnp.bfloat16),
            pltpu.VMEM((CH * 16, COLS), jnp.bfloat16),
            pltpu.VMEM((CH, TILE, TILE), jnp.bfloat16),
            pltpu.VMEM((CH, LAGS, TILE), jnp.float32),
            pltpu.VMEM((2, CH, TILE, LAGS), jnp.bfloat16),
            pltpu.SemaphoreType.DMA((STEPS,)),
            pltpu.SemaphoreType.DMA((STEPS, 2, 8)),
            pltpu.SemaphoreType.DMA((STEPS, 15)),
            pltpu.SemaphoreType.DMA((16,)),
            pltpu.SemaphoreType.DMA((16,)),
        ],
        compiler_params=pltpu.CompilerParams(
            collective_id=0, has_side_effects=True, vmem_limit_bytes=60 << 20
        ),
        name="pairs",
    )(own, part, table)


def on_device(spectra, partner):
    whitened = whiten(spectra)
    rows = whitened.reshape(CH, WINDOWS, 2, INNER, COLS)
    rows = jnp.transpose(rows, (4, 0, 2, 3, 1)).reshape(COLS, CH, COLS)
    swap = [(0, 0), (1, 2), (2, 1), (3, 3)]
    own = lax.ppermute(rows, ("core", "ylo"), swap)
    groups = ("x", "yh", "ylo")
    spread = lax.all_to_all(
        own.reshape(16, COLS // 16, CH, COLS), groups, split_axis=0, concat_axis=0, tiled=True
    )
    ordered = jnp.take(spread, partner, axis=0)
    part = lax.all_to_all(ordered, groups, split_axis=0, concat_axis=0, tiled=True)
    return correlate_pairs(own, part.reshape(COLS, CH, COLS), lag_rows())


def solution(mesh):
    split = Mesh(mesh.devices.reshape(4, 2, 2, 2, 8), AXES)
    return jax.shard_map(
        on_device,
        mesh=split,
        in_specs=(P(AXES, None, None), P()),
        out_specs=P(AXES, None, None),
        check_vma=False,
    )
```

```python
import functools
import math

import jax
import jax.numpy as jnp
from jax import lax
from jax.experimental import pallas as pl
from jax.experimental.pallas import tpu as pltpu
from jax.sharding import Mesh
from jax.sharding import PartitionSpec as P

LAGS = 128
HALF = 64
FREQS = 1024
WINDOWS = 8
CH = 32
COLS = 128
INNER = 8
CHUNK = 16
STEPS = COLS // CHUNK
TILE = 256
GROUP_COLS = 4
GROUP_CH = 8
AXES = ("x", "yh", "core", "ylo", "z")
MESH = pl.DeviceIdType.MESH

SLOT = {0: 0, 1: 1, -1: 2, 2: 3, -2: 4, 3: 5, -3: 6, 4: 7}
DIST = {slot: dist for dist, slot in SLOT.items()}


def band_matrix():
    positions = jnp.arange(FREQS, dtype=jnp.int32)
    distance = jnp.abs(positions[:, None] - positions[None, :])
    band_ones = (distance <= HALF).astype(jnp.float32)
    counts = (
        jnp.minimum(positions + HALF, FREQS - 1) - jnp.maximum(positions - HALF, 0) + 1
    ).astype(jnp.float32)
    return band_ones, counts


def whiten(spectra):
    real_part = spectra[:, :, :FREQS].astype(jnp.float32)
    imag_part = spectra[:, :, FREQS:].astype(jnp.float32)
    power_sum = jnp.sum(real_part * real_part + imag_part * imag_part, axis=1)
    band_ones, counts = band_matrix()
    smoothed = jnp.dot(power_sum, band_ones, precision=lax.Precision.HIGHEST)
    average = smoothed / (counts * WINDOWS)
    inverse_amp = 1.0 / jnp.sqrt(average + 1e-05)
    factor = jnp.concatenate([inverse_amp, inverse_amp], axis=1)
    return (spectra.astype(jnp.float32) * factor[:, None, :]).astype(jnp.bfloat16)


def lag_rows():
    lag_values = jnp.arange(LAGS, dtype=jnp.int32) - LAGS // 2
    columns = jnp.arange(COLS, dtype=jnp.int32).reshape(STEPS, CHUNK)
    freq = columns[:, :, None] + COLS * jnp.arange(INNER, dtype=jnp.int32)[None, None, :]
    residue = jnp.mod(freq[:, None, :, :] * lag_values[None, :, None, None], 2 * FREQS)
    angles = jnp.pi * residue.astype(jnp.float32) / FREQS
    norm_factor = 1.0 / math.sqrt(WINDOWS * FREQS)
    table = jnp.stack([jnp.cos(angles) * norm_factor, -jnp.sin(angles) * norm_factor], axis=3)
    return table.reshape(STEPS, LAGS, CHUNK * 2 * INNER).astype(jnp.bfloat16)


def pair_kernel(
    own_ref, part_ref, lag_ref, out_ref,
    x_rows, xs_rows, gathered, left, cross, total, result,
    own_sem, recv_sem, send_sem, out_send, out_recv,
):
    core = lax.axis_index("core")
    ylo = lax.axis_index("ylo")
    z = lax.axis_index("z")
    up = lax.rem(z + 1, 8)
    down = lax.rem(z + 7, 8)
    moved = core != ylo

    barrier = pltpu.get_barrier_semaphore()
    pl.semaphore_signal(barrier, inc=1, device_id={"z": up}, device_id_type=MESH)
    pl.semaphore_signal(barrier, inc=1, device_id={"z": down}, device_id_type=MESH)
    pl.semaphore_signal(barrier, inc=1, device_id={"core": 1 - core}, device_id_type=MESH)

    @pl.when(moved)
    def _():
        pl.semaphore_signal(
            barrier, inc=1, device_id={"core": ylo, "ylo": core}, device_id_type=MESH
        )
        pl.semaphore_wait(barrier, 4)

    @pl.when(jnp.logical_not(moved))
    def _():
        pl.semaphore_wait(barrier, 3)

    def columns(c):
        return pl.ds(pl.multiple_of(c * CHUNK, CHUNK), CHUNK)

    def place(c, dist, member):
        start = SLOT[dist] * 64 + member * 32
        return gathered.at[columns(c), pl.ds(pl.multiple_of(start, 32), 32), :]

    def source(c, dist):
        return part_ref.at[columns(c)] if dist == 0 else place(c, dist, core)

    def hop(c, dist, step):
        landed = 4 if dist + step == -4 else dist + step
        return pltpu.make_async_remote_copy(
            src_ref=source(c, dist),
            dst_ref=place(c, landed, core),
            send_sem=send_sem.at[c, SLOT[landed] - 1],
            recv_sem=recv_sem.at[c, 0, SLOT[landed]],
            device_id={"z": down if step == 1 else up},
            device_id_type=MESH,
        )

    def across(c, dist):
        return pltpu.make_async_remote_copy(
            src_ref=source(c, dist),
            dst_ref=place(c, dist, core),
            send_sem=send_sem.at[c, 7 + SLOT[dist]],
            recv_sem=recv_sem.at[c, 1, SLOT[dist]],
            device_id={"core": 1 - core},
            device_id_type=MESH,
        )

    def own_copy(c):
        return pltpu.make_async_copy(part_ref.at[columns(c)], place(c, 0, core), own_sem.at[c])

    def result_pieces(tile):
        for piece in range(4):
            from_z = lax.rem(z + DIST[tile * 4 + piece] + 8, 8)
            for member in range(2):
                rows = pl.ds(piece * 64 + member * 32, 32)
                target = pl.ds(pl.multiple_of((member * 8 + from_z) * 32, 32), 32)
                yield tile * 8 + piece * 2 + member, result.at[tile, :, rows, :], target

    def result_remote(index, src, target):
        return pltpu.make_async_remote_copy(
            src_ref=src, dst_ref=out_ref.at[:, target, :],
            send_sem=out_send.at[index], recv_sem=out_recv.at[index],
            device_id={"core": ylo, "ylo": core}, device_id_type=MESH,
        )

    def result_local(index, src, target):
        return pltpu.make_async_copy(src, out_ref.at[:, target, :], out_send.at[index])

    def send_result(tile):
        @pl.when(moved)
        def _():
            for piece in result_pieces(tile):
                result_remote(*piece).start()

        @pl.when(jnp.logical_not(moved))
        def _():
            for piece in result_pieces(tile):
                result_local(*piece).start()

    lane = lax.broadcasted_iota(jnp.int32, (INNER, COLS), 1)
    row = lax.broadcasted_iota(jnp.int32, (INNER, COLS), 0)
    mask = lax.rem(lane // WINDOWS, INNER) == row
    sign = jnp.where(lax.broadcasted_iota(jnp.int32, (CH, COLS), 1) < 64, 1.0, -1.0)

    def load_rows(column):
        value = own_ref[column].astype(jnp.float32)
        x_rows[column] = value
        xs_rows[column] = pltpu.roll(value, 64, 1) * sign

    def cross_column(c, i, lane_slot, tile):
        column = c * CHUNK + i
        for a in range(CH):
            re_row = jnp.broadcast_to(x_rows[column, pl.ds(a, 1), :], (INNER, COLS))
            im_row = jnp.broadcast_to(xs_rows[column, pl.ds(a, 1), :], (INNER, COLS))
            block = jnp.concatenate(
                [jnp.where(mask, re_row, 0.0), jnp.where(mask, im_row, 0.0)], axis=0
            )
            left[lane_slot, pl.ds(a * 16, 16), :] = block.astype(jnp.bfloat16)
        right = gathered[column, pl.ds(pl.multiple_of(tile * TILE, TILE), TILE), :]
        product = lax.dot_general(
            left[lane_slot], right, (((1,), (1,)), ((), ())), preferred_element_type=jnp.float32
        )
        cross[:, pl.ds(pl.multiple_of(i * 16, 16), 16), :] = product.astype(
            jnp.bfloat16
        ).reshape(CH, 16, TILE)

    def lag_channel(c, a):
        product = jnp.dot(lag_ref[c], cross[a], preferred_element_type=jnp.float32)
        total[a] = jnp.where(c > 0, total[a], 0.0) + product

    def compute(c, tile):
        @pl.loop(0, CHUNK // GROUP_COLS)
        def _(i):
            for u in range(GROUP_COLS):
                cross_column(c, i * GROUP_COLS + u, u, tile)

        @pl.loop(0, CH // GROUP_CH)
        def _(i):
            for u in range(GROUP_CH):
                lag_channel(c, i * GROUP_CH + u)

        @pl.when(c == STEPS - 1)
        def _():
            @pl.loop(0, CH // 4)
            def _(i):
                for u in range(4):
                    result[tile, i * 4 + u] = total[i * 4 + u].T.astype(jnp.bfloat16)

    def inside(c):
        return jnp.logical_and(c >= 0, c < STEPS)

    @pl.loop(0, 2 * STEPS + 3)
    def _(tick):
        t = tick - 3

        @pl.when(inside(t + 3))
        def _():
            c = t + 3
            own_copy(c).start()
            hop(c, 0, 1).start()
            hop(c, 0, -1).start()
            across(c, 0).start()

        @pl.when(inside(t + 2))
        def _():
            c = t + 2
            hop(c, 0, 1).wait_recv()
            hop(c, 1, 1).start()
            hop(c, 0, -1).wait_recv()
            hop(c, -1, -1).start()
            across(c, 1).start()
            across(c, -1).start()

        @pl.when(inside(t + 1))
        def _():
            c = t + 1
            hop(c, 1, 1).wait_recv()
            across(c, 2).start()
            hop(c, -1, -1).wait_recv()
            across(c, -2).start()

        @pl.when(inside(t - 5))
        def _():
            c = t - 5
            hop(c, 2, 1).start()
            hop(c, -2, -1).start()

        @pl.when(inside(t - 6))
        def _():
            c = t - 6
            hop(c, 2, 1).wait_recv()
            hop(c, -2, -1).wait_recv()

            @pl.when(lax.rem(c, 2) == 0)
            def _():
                hop(c, 3, 1).start()

            @pl.when(lax.rem(c, 2) == 1)
            def _():
                hop(c, -3, -1).start()

            across(c, 3).start()
            across(c, -3).start()

        @pl.when(inside(t - 7))
        def _():
            c = t - 7
            hop(c, 3, 1).wait_recv()
            across(c, 4).start()

        @pl.when(t < 0)
        def _():
            @pl.loop(0, 43)
            def _(i):
                load_rows(jnp.minimum((t + 3) * 43 + i, COLS - 1))

        @pl.when(inside(t))
        def _():
            own_copy(t).wait()
            for dist in (0, 1, -1, 2):
                across(t, dist).wait_recv()
            compute(t, 0)

        @pl.when(t == STEPS)
        def _():
            send_result(0)

        @pl.when(t >= STEPS)
        def _():
            for dist in (-2, 3, -3, 4):
                across(t - STEPS, dist).wait_recv()
            compute(t - STEPS, 1)

    send_result(1)

    @pl.loop(0, STEPS)
    def _(c):
        for dist, step in ((0, 1), (0, -1), (1, 1), (-1, -1), (2, 1), (-2, -1), (3, 1)):
            hop(c, dist, step).wait_send()
        for dist in DIST.values():
            across(c, dist).wait_send()

    @pl.when(moved)
    def _():
        for tile in range(2):
            for piece in result_pieces(tile):
                result_remote(*piece).wait()

    @pl.when(jnp.logical_not(moved))
    def _():
        for tile in range(2):
            for piece in result_pieces(tile):
                result_local(*piece).wait()


def correlate_pairs(own, part, table):
    return pl.pallas_call(
        pair_kernel,
        out_shape=jax.ShapeDtypeStruct((CH, 16 * CH, LAGS), jnp.bfloat16),
        in_specs=[
            pl.BlockSpec(memory_space=pltpu.VMEM),
            pl.BlockSpec(memory_space=pl.ANY),
            pl.BlockSpec(memory_space=pltpu.VMEM),
        ],
        out_specs=pl.BlockSpec(memory_space=pl.ANY),
        scratch_shapes=[
            pltpu.VMEM((COLS, CH, COLS), jnp.float32),
            pltpu.VMEM((COLS, CH, COLS), jnp.float32),
            pltpu.VMEM((COLS, 16 * CH, COLS), jnp.bfloat16),
            pltpu.VMEM((GROUP_COLS, CH * 16, COLS), jnp.bfloat16),
            pltpu.VMEM((CH, TILE, TILE), jnp.bfloat16),
            pltpu.VMEM((CH, LAGS, TILE), jnp.float32),
            pltpu.VMEM((2, CH, TILE, LAGS), jnp.bfloat16),
            pltpu.SemaphoreType.DMA((STEPS,)),
            pltpu.SemaphoreType.DMA((STEPS, 2, 8)),
            pltpu.SemaphoreType.DMA((STEPS, 15)),
            pltpu.SemaphoreType.DMA((16,)),
            pltpu.SemaphoreType.DMA((16,)),
        ],
        compiler_params=pltpu.CompilerParams(
            collective_id=0, has_side_effects=True, vmem_limit_bytes=60 << 20
        ),
        name="pairs",
    )(own, part, table)


def on_device(spectra, partner):
    whitened = whiten(spectra)
    rows = whitened.reshape(CH, WINDOWS, 2, INNER, COLS)
    rows = jnp.transpose(rows, (4, 0, 2, 3, 1)).reshape(COLS, CH, COLS)
    swap = [(0, 0), (1, 2), (2, 1), (3, 3)]
    own = lax.ppermute(rows, ("core", "ylo"), swap)
    groups = ("x", "yh", "ylo")
    spread = lax.all_to_all(
        own.reshape(16, COLS // 16, CH, COLS), groups, split_axis=0, concat_axis=0, tiled=True
    )
    ordered = jnp.take(spread, partner, axis=0)
    part = lax.all_to_all(ordered, groups, split_axis=0, concat_axis=0, tiled=True)
    return correlate_pairs(own, part.reshape(COLS, CH, COLS), lag_rows())


def solution(mesh):
    split = Mesh(mesh.devices.reshape(4, 2, 2, 2, 8), AXES)
    return jax.shard_map(
        on_device,
        mesh=split,
        in_specs=(P(AXES, None, None), P()),
        out_specs=P(AXES, None, None),
        check_vma=False,
    )
```

```python
import functools
import math

import jax
import jax.numpy as jnp
import numpy as np
from jax import lax
from jax.experimental import pallas as pl
from jax.experimental.pallas import tpu as pltpu
from jax.sharding import Mesh
from jax.sharding import PartitionSpec as P

LAGS = 128
HALF = 64
FREQS = 1024
WINDOWS = 8
CH = 32
COLS = 128
INNER = 8
CHUNK = 16
STEPS = COLS // CHUNK
TILE = 256
GROUP_COLS = 4
GROUP_CH = 8
AXES = ("x", "yh", "core", "ylo", "z")
MESH = pl.DeviceIdType.MESH

SLOT = {0: 0, 1: 1, -1: 2, 2: 3, -2: 4, 3: 5, -3: 6, 4: 7}
DIST = {slot: dist for dist, slot in SLOT.items()}


def band_matrix():
    positions = jnp.arange(FREQS, dtype=jnp.int32)
    distance = jnp.abs(positions[:, None] - positions[None, :])
    band_ones = (distance <= HALF).astype(jnp.float32)
    counts = (
        jnp.minimum(positions + HALF, FREQS - 1) - jnp.maximum(positions - HALF, 0) + 1
    ).astype(jnp.float32)
    return band_ones, counts


def whiten(spectra):
    real_part = spectra[:, :, :FREQS].astype(jnp.float32)
    imag_part = spectra[:, :, FREQS:].astype(jnp.float32)
    power_sum = jnp.sum(real_part * real_part + imag_part * imag_part, axis=1)
    band_ones, counts = band_matrix()
    smoothed = jnp.dot(power_sum, band_ones, precision=lax.Precision.HIGHEST)
    average = smoothed / (counts * WINDOWS)
    inverse_amp = 1.0 / jnp.sqrt(average + 1e-05)
    factor = jnp.concatenate([inverse_amp, inverse_amp], axis=1)
    return (spectra.astype(jnp.float32) * factor[:, None, :]).astype(jnp.bfloat16)


def lag_rows():
    lag_values = np.arange(LAGS) - LAGS // 2
    columns = np.arange(COLS).reshape(STEPS, CHUNK)
    freq = columns[:, :, None] + COLS * np.arange(INNER)[None, None, :]
    residue = np.mod(freq[:, None, :, :] * lag_values[None, :, None, None], 2 * FREQS)
    angles = np.pi * residue / FREQS
    norm_factor = 1.0 / math.sqrt(WINDOWS * FREQS)
    table = np.stack([np.cos(angles) * norm_factor, -np.sin(angles) * norm_factor], axis=3)
    return table.reshape(STEPS, LAGS, CHUNK * 2 * INNER).astype(jnp.bfloat16)


def pair_kernel(
    partner_ref, rows_ref, lag_ref, out_ref,
    spread, ordered, own, x_rows, xs_rows, gathered, left, cross, total, result,
    local_sem, spread_send, spread_recv, own_send, own_recv, part_send, part_recv,
    recv_sem, send_sem, out_send, out_recv,
):
    x = lax.axis_index("x")
    yh = lax.axis_index("yh")
    core = lax.axis_index("core")
    ylo = lax.axis_index("ylo")
    z = lax.axis_index("z")
    up = lax.rem(z + 1, 8)
    down = lax.rem(z + 7, 8)
    moved = core != ylo
    chip = x * 2 + yh
    group = chip * 2 + core
    mirror = {"core": ylo, "ylo": core}

    barrier = pltpu.get_barrier_semaphore()
    plane = group * 2 + ylo
    for i in range(1, 32):
        other = lax.rem(plane + i, 32)
        where = {
            "x": other // 8, "yh": lax.rem(other // 4, 2),
            "core": lax.rem(other // 2, 2), "ylo": lax.rem(other, 2),
        }
        pl.semaphore_signal(barrier, inc=1, device_id=where, device_id_type=MESH)
    pl.semaphore_signal(barrier, inc=1, device_id={"z": up}, device_id_type=MESH)
    pl.semaphore_signal(barrier, inc=1, device_id={"z": down}, device_id_type=MESH)
    pl.semaphore_wait(barrier, 33)

    def share(t):
        to = lax.rem(group + t, 16)
        return pltpu.make_async_remote_copy(
            src_ref=rows_ref.at[pl.ds(pl.multiple_of(to * 8, 8), 8)],
            dst_ref=spread.at[group],
            send_sem=spread_send.at[t],
            recv_sem=spread_recv.at[group],
            device_id={"x": to // 4, "yh": lax.rem(to // 2, 2), "core": lax.rem(to, 2)},
            device_id_type=MESH,
        )

    def share_from(t):
        source = lax.rem(group + t, 16)
        return pltpu.make_async_remote_copy(
            src_ref=rows_ref.at[pl.ds(0, 8)],
            dst_ref=spread.at[source],
            send_sem=spread_send.at[t],
            recv_sem=spread_recv.at[source],
            device_id={"core": 1 - core},
            device_id_type=MESH,
        )

    own_share = pltpu.make_async_copy(
        rows_ref.at[pl.ds(pl.multiple_of(group * 8, 8), 8)], spread.at[group], local_sem.at[0]
    )
    own_swap = pltpu.make_async_remote_copy(
        src_ref=rows_ref, dst_ref=own, send_sem=own_send, recv_sem=own_recv,
        device_id=mirror, device_id_type=MESH,
    )
    own_stay = pltpu.make_async_copy(rows_ref, own, local_sem.at[1])

    own_share.start()
    for t in range(1, 16):
        share(t).start()

    @pl.when(moved)
    def _():
        own_swap.start()

    @pl.when(jnp.logical_not(moved))
    def _():
        own_stay.start()

    own_share.wait()
    for t in range(1, 16):
        share_from(t).wait_recv()

    for g in range(16):
        ordered[g] = spread[partner_ref[g]]

    def columns(c):
        step = lax.rem(c + chip, STEPS)
        return pl.ds(pl.multiple_of(step * CHUNK, CHUNK), CHUNK)

    def place(c, dist, member):
        start = SLOT[dist] * 64 + member * 32
        return gathered.at[columns(c), pl.ds(pl.multiple_of(start, 32), 32), :]

    def share_place(source, member):
        cols = pl.ds(pl.multiple_of(source * 8, 8), 8)
        return gathered.at[cols, pl.ds(pl.multiple_of(member * 32, 32), 32), :]

    def give(t, member):
        to = lax.rem(chip + 8 - t, 8)
        return pltpu.make_async_remote_copy(
            src_ref=ordered.at[to * 2 + member],
            dst_ref=share_place(group, ylo),
            send_sem=part_send.at[t * 2 + member],
            recv_sem=part_recv.at[group],
            device_id={"x": to // 2, "yh": lax.rem(to, 2), "core": ylo, "ylo": member},
            device_id_type=MESH,
        )

    def keep(member):
        return pltpu.make_async_copy(
            ordered.at[chip * 2 + member], share_place(group, ylo), local_sem.at[2]
        )

    def take(c, source_core):
        source = lax.rem(chip + c, 8) * 2 + source_core
        return pltpu.make_async_remote_copy(
            src_ref=ordered.at[0],
            dst_ref=share_place(source, core),
            send_sem=part_send.at[0],
            recv_sem=part_recv.at[source],
            device_id={"core": 1 - core},
            device_id_type=MESH,
        )

    for member in range(2):
        stays = jnp.logical_and(jnp.logical_not(moved), ylo == member)

        @pl.when(stays)
        def _():
            keep(member).start()

        @pl.when(jnp.logical_not(stays))
        def _():
            give(0, member).start()

    for t in range(1, 8):
        for member in range(2):
            give(t, member).start()

    def wait_part(c):
        for source_core in range(2):
            stays = jnp.logical_and(
                c == 0, jnp.logical_and(jnp.logical_not(moved), core == source_core)
            )

            @pl.when(stays)
            def _():
                keep(source_core).wait()

            @pl.when(jnp.logical_not(stays))
            def _():
                take(c, source_core).wait_recv()

    def hop(c, dist, step):
        landed = 4 if dist + step == -4 else dist + step
        return pltpu.make_async_remote_copy(
            src_ref=place(c, dist, core),
            dst_ref=place(c, landed, core),
            send_sem=send_sem.at[c, SLOT[landed] - 1],
            recv_sem=recv_sem.at[c, 0, SLOT[landed]],
            device_id={"z": down if step == 1 else up},
            device_id_type=MESH,
        )

    def across(c, dist):
        return pltpu.make_async_remote_copy(
            src_ref=place(c, dist, core),
            dst_ref=place(c, dist, core),
            send_sem=send_sem.at[c, 7 + SLOT[dist]],
            recv_sem=recv_sem.at[c, 1, SLOT[dist]],
            device_id={"core": 1 - core},
            device_id_type=MESH,
        )

    def across_in(c, dist):
        return pltpu.make_async_remote_copy(
            src_ref=place(c, dist, core),
            dst_ref=place(c, dist, 1 - core),
            send_sem=send_sem.at[c, 7 + SLOT[dist]],
            recv_sem=recv_sem.at[c, 1, SLOT[dist]],
            device_id={"core": 1 - core},
            device_id_type=MESH,
        )

    def result_pieces(tile):
        for piece in range(4):
            from_z = lax.rem(z + DIST[tile * 4 + piece] + 8, 8)
            for member in range(2):
                rows = pl.ds(piece * 64 + member * 32, 32)
                target = pl.ds(pl.multiple_of((member * 8 + from_z) * 32, 32), 32)
                yield tile * 8 + piece * 2 + member, result.at[tile, :, rows, :], target

    def result_remote(index, src, target):
        return pltpu.make_async_remote_copy(
            src_ref=src, dst_ref=out_ref.at[:, target, :],
            send_sem=out_send.at[index], recv_sem=out_recv.at[index],
            device_id=mirror, device_id_type=MESH,
        )

    def result_local(index, src, target):
        return pltpu.make_async_copy(src, out_ref.at[:, target, :], out_send.at[index])

    def send_result(tile):
        @pl.when(moved)
        def _():
            for piece in result_pieces(tile):
                result_remote(*piece).start()

        @pl.when(jnp.logical_not(moved))
        def _():
            for piece in result_pieces(tile):
                result_local(*piece).start()

    lane = lax.broadcasted_iota(jnp.int32, (INNER, COLS), 1)
    row = lax.broadcasted_iota(jnp.int32, (INNER, COLS), 0)
    mask = lax.rem(lane // WINDOWS, INNER) == row
    sign = jnp.where(lax.broadcasted_iota(jnp.int32, (CH, COLS), 1) < 64, 1.0, -1.0)

    def load_rows(column):
        value = own[column].astype(jnp.float32)
        x_rows[column] = value
        xs_rows[column] = pltpu.roll(value, 64, 1) * sign

    def cross_column(c, i, lane_slot, tile):
        column = lax.rem(c + chip, STEPS) * CHUNK + i
        for a in range(CH):
            re_row = jnp.broadcast_to(x_rows[column, pl.ds(a, 1), :], (INNER, COLS))
            im_row = jnp.broadcast_to(xs_rows[column, pl.ds(a, 1), :], (INNER, COLS))
            block = jnp.concatenate(
                [jnp.where(mask, re_row, 0.0), jnp.where(mask, im_row, 0.0)], axis=0
            )
            left[lane_slot, pl.ds(a * 16, 16), :] = block.astype(jnp.bfloat16)
        right = gathered[column, pl.ds(pl.multiple_of(tile * TILE, TILE), TILE), :]
        product = lax.dot_general(
            left[lane_slot], right, (((1,), (1,)), ((), ())), preferred_element_type=jnp.float32
        )
        cross[:, pl.ds(pl.multiple_of(i * 16, 16), 16), :] = product.astype(
            jnp.bfloat16
        ).reshape(CH, 16, TILE)

    def lag_channel(c, a):
        product = jnp.dot(lag_ref[lax.rem(c + chip, STEPS)], cross[a], preferred_element_type=jnp.float32)
        total[a] = jnp.where(c > 0, total[a], 0.0) + product

    def compute(c, tile):
        @pl.loop(0, CHUNK // GROUP_COLS)
        def _(i):
            for u in range(GROUP_COLS):
                cross_column(c, i * GROUP_COLS + u, u, tile)

        @pl.loop(0, CH // GROUP_CH)
        def _(i):
            for u in range(GROUP_CH):
                lag_channel(c, i * GROUP_CH + u)

        @pl.when(c == STEPS - 1)
        def _():
            @pl.loop(0, CH // 4)
            def _(i):
                for u in range(4):
                    result[tile, i * 4 + u] = total[i * 4 + u].T.astype(jnp.bfloat16)

    def inside(c):
        return jnp.logical_and(c >= 0, c < STEPS)

    @pl.loop(0, 2 * STEPS + 5)
    def _(tick):
        t = tick - 5

        @pl.when(inside(t + 3))
        def _():
            c = t + 3
            hop(c, 0, 1).wait_recv()
            hop(c, 1, 1).start()
            hop(c, 0, -1).wait_recv()
            hop(c, -1, -1).start()
            across(c, 1).start()
            across(c, -1).start()

        @pl.when(inside(t + 5))
        def _():
            c = t + 5
            wait_part(c)
            hop(c, 0, 1).start()
            hop(c, 0, -1).start()
            across(c, 0).start()

        @pl.when(inside(t + 1))
        def _():
            c = t + 1
            hop(c, 1, 1).wait_recv()
            across(c, 2).start()
            hop(c, -1, -1).wait_recv()
            across(c, -2).start()

        @pl.when(inside(t - 3))
        def _():
            c = t - 3
            hop(c, 2, 1).start()
            hop(c, -2, -1).start()

        @pl.when(inside(t - 5))
        def _():
            c = t - 5
            hop(c, 2, 1).wait_recv()
            hop(c, -2, -1).wait_recv()

            @pl.when(lax.rem(c, 2) == 0)
            def _():
                hop(c, 3, 1).start()

            @pl.when(lax.rem(c, 2) == 1)
            def _():
                hop(c, -3, -1).start()

            across(c, 3).start()
            across(c, -3).start()

        @pl.when(inside(t - 7))
        def _():
            c = t - 7
            hop(c, 3, 1).wait_recv()
            across(c, 4).start()

        @pl.when(t == -3)
        def _():
            @pl.when(moved)
            def _():
                own_swap.wait_recv()

            @pl.when(jnp.logical_not(moved))
            def _():
                own_stay.wait()

        @pl.when(jnp.logical_and(t >= -3, t < 0))
        def _():
            @pl.loop(0, 43)
            def _(i):
                load_rows(jnp.minimum((t + 3) * 43 + i, COLS - 1))

        @pl.when(inside(t))
        def _():
            for dist in (0, 1, -1, 2):
                across_in(t, dist).wait_recv()
            compute(t, 0)

        @pl.when(t == STEPS)
        def _():
            send_result(0)

        @pl.when(t >= STEPS)
        def _():
            for dist in (-2, 3, -3, 4):
                across_in(t - STEPS, dist).wait_recv()
            compute(t - STEPS, 1)

    send_result(1)

    for t in range(1, 16):
        share(t).wait_send()

    @pl.when(moved)
    def _():
        own_swap.wait_send()

    for member in range(2):
        @pl.when(jnp.logical_or(moved, ylo != member))
        def _():
            give(0, member).wait_send()

    for t in range(1, 8):
        for member in range(2):
            give(t, member).wait_send()

    @pl.loop(0, STEPS)
    def _(c):
        for dist, step in ((0, 1), (0, -1), (1, 1), (-1, -1), (2, 1), (-2, -1), (3, 1)):
            hop(c, dist, step).wait_send()
        for dist in DIST.values():
            across(c, dist).wait_send()

    @pl.when(moved)
    def _():
        for tile in range(2):
            for piece in result_pieces(tile):
                result_remote(*piece).wait()

    @pl.when(jnp.logical_not(moved))
    def _():
        for tile in range(2):
            for piece in result_pieces(tile):
                result_local(*piece).wait()


def correlate_pairs(partner, rows, table):
    return pl.pallas_call(
        pair_kernel,
        out_shape=jax.ShapeDtypeStruct((CH, 16 * CH, LAGS), jnp.bfloat16),
        in_specs=[
            pl.BlockSpec(memory_space=pltpu.SMEM),
            pl.BlockSpec(memory_space=pl.ANY),
            pl.BlockSpec(memory_space=pltpu.VMEM),
        ],
        out_specs=pl.BlockSpec(memory_space=pl.ANY),
        scratch_shapes=[
            pltpu.VMEM((16, 8, CH, COLS), jnp.bfloat16),
            pltpu.VMEM((16, 8, CH, COLS), jnp.bfloat16),
            pltpu.VMEM((COLS, CH, COLS), jnp.bfloat16),
            pltpu.VMEM((COLS, CH, COLS), jnp.float32),
            pltpu.VMEM((COLS, CH, COLS), jnp.float32),
            pltpu.VMEM((COLS, 16 * CH, COLS), jnp.bfloat16),
            pltpu.VMEM((GROUP_COLS, CH * 16, COLS), jnp.bfloat16),
            pltpu.VMEM((CH, TILE, TILE), jnp.bfloat16),
            pltpu.VMEM((CH, LAGS, TILE), jnp.float32),
            pltpu.VMEM((2, CH, TILE, LAGS), jnp.bfloat16),
            pltpu.SemaphoreType.DMA((3,)),
            pltpu.SemaphoreType.DMA((16,)),
            pltpu.SemaphoreType.DMA((16,)),
            pltpu.SemaphoreType.DMA,
            pltpu.SemaphoreType.DMA,
            pltpu.SemaphoreType.DMA((16,)),
            pltpu.SemaphoreType.DMA((16,)),
            pltpu.SemaphoreType.DMA((STEPS, 2, 8)),
            pltpu.SemaphoreType.DMA((STEPS, 15)),
            pltpu.SemaphoreType.DMA((16,)),
            pltpu.SemaphoreType.DMA((16,)),
        ],
        compiler_params=pltpu.CompilerParams(
            collective_id=0, has_side_effects=True, vmem_limit_bytes=60 << 20
        ),
        name="pairs",
    )(partner, rows, table)


def on_device(spectra, partner):
    whitened = whiten(spectra)
    rows = whitened.reshape(CH, WINDOWS, 2, INNER, COLS)
    rows = jnp.transpose(rows, (4, 0, 2, 3, 1)).reshape(COLS, CH, COLS)
    return correlate_pairs(partner, rows, jnp.asarray(lag_rows()))


def solution(mesh):
    split = Mesh(mesh.devices.reshape(4, 2, 2, 2, 8), AXES)
    return jax.shard_map(
        on_device,
        mesh=split,
        in_specs=(P(AXES, None, None), P()),
        out_specs=P(AXES, None, None),
        check_vma=False,
    )
```

```python
import functools
import math

import jax
import jax.numpy as jnp
import numpy as np
from jax import lax
from jax.experimental import pallas as pl
from jax.experimental.pallas import tpu as pltpu
from jax.sharding import Mesh
from jax.sharding import PartitionSpec as P

LAGS = 128
HALF = 64
FREQS = 1024
WINDOWS = 8
CH = 32
COLS = 128
INNER = 8
CHUNK = 16
STEPS = COLS // CHUNK
TILES = ((0, 256), (256, 128), (384, 128))
TILE = 256
GROUP_COLS = 8
GROUP_CH = 16
AXES = ("x", "yh", "core", "ylo", "z")
MESH = pl.DeviceIdType.MESH

SLOT = {0: 0, 1: 1, -1: 2, 2: 3, -2: 4, 3: 5, -3: 6, 4: 7}
DIST = {slot: dist for dist, slot in SLOT.items()}


def band_matrix():
    positions = jnp.arange(FREQS, dtype=jnp.int32)
    distance = jnp.abs(positions[:, None] - positions[None, :])
    band_ones = (distance <= HALF).astype(jnp.float32)
    counts = (
        jnp.minimum(positions + HALF, FREQS - 1) - jnp.maximum(positions - HALF, 0) + 1
    ).astype(jnp.float32)
    return band_ones, counts


def whiten(spectra):
    real_part = spectra[:, :, :FREQS].astype(jnp.float32)
    imag_part = spectra[:, :, FREQS:].astype(jnp.float32)
    power_sum = jnp.sum(real_part * real_part + imag_part * imag_part, axis=1)
    band_ones, counts = band_matrix()
    smoothed = jnp.dot(power_sum, band_ones, precision=lax.Precision.HIGHEST)
    average = smoothed / (counts * WINDOWS)
    inverse_amp = 1.0 / jnp.sqrt(average + 1e-05)
    factor = jnp.concatenate([inverse_amp, inverse_amp], axis=1)
    return (spectra.astype(jnp.float32) * factor[:, None, :]).astype(jnp.bfloat16)


def lag_rows():
    lag_values = np.arange(LAGS) - LAGS // 2
    columns = np.arange(COLS).reshape(STEPS, CHUNK)
    freq = columns[:, :, None] + COLS * np.arange(INNER)[None, None, :]
    residue = np.mod(freq[:, None, :, :] * lag_values[None, :, None, None], 2 * FREQS)
    angles = np.pi * residue / FREQS
    norm_factor = 1.0 / math.sqrt(WINDOWS * FREQS)
    table = np.stack([np.cos(angles) * norm_factor, -np.sin(angles) * norm_factor], axis=3)
    return table.reshape(STEPS, LAGS, CHUNK * 2 * INNER).astype(jnp.bfloat16)


def pair_kernel(
    partner_ref, rows_ref, lag_ref, out_ref,
    spread, ordered, own, x_rows, xs_rows, gathered, left, cross, total, result,
    local_sem, spread_send, spread_recv, own_send, own_recv, part_send, part_recv,
    recv_sem, send_sem, out_send, out_recv,
):
    x = lax.axis_index("x")
    yh = lax.axis_index("yh")
    core = lax.axis_index("core")
    ylo = lax.axis_index("ylo")
    z = lax.axis_index("z")
    up = lax.rem(z + 1, 8)
    down = lax.rem(z + 7, 8)
    moved = core != ylo
    chip = x * 2 + yh
    group = chip * 2 + core
    mirror = {"core": ylo, "ylo": core}

    barrier = pltpu.get_barrier_semaphore()
    plane = group * 2 + ylo
    for i in range(1, 32):
        other = lax.rem(plane + i, 32)
        where = {
            "x": other // 8, "yh": lax.rem(other // 4, 2),
            "core": lax.rem(other // 2, 2), "ylo": lax.rem(other, 2),
        }
        pl.semaphore_signal(barrier, inc=1, device_id=where, device_id_type=MESH)
    pl.semaphore_signal(barrier, inc=1, device_id={"z": up}, device_id_type=MESH)
    pl.semaphore_signal(barrier, inc=1, device_id={"z": down}, device_id_type=MESH)
    pl.semaphore_wait(barrier, 33)

    def share(t):
        to = lax.rem(group + t, 16)
        return pltpu.make_async_remote_copy(
            src_ref=rows_ref.at[pl.ds(pl.multiple_of(to * 8, 8), 8)],
            dst_ref=spread.at[group],
            send_sem=spread_send.at[t],
            recv_sem=spread_recv.at[group],
            device_id={"x": to // 4, "yh": lax.rem(to // 2, 2), "core": lax.rem(to, 2)},
            device_id_type=MESH,
        )

    def share_from(t):
        source = lax.rem(group + t, 16)
        return pltpu.make_async_remote_copy(
            src_ref=rows_ref.at[pl.ds(0, 8)],
            dst_ref=spread.at[source],
            send_sem=spread_send.at[t],
            recv_sem=spread_recv.at[source],
            device_id={"core": 1 - core},
            device_id_type=MESH,
        )

    own_share = pltpu.make_async_copy(
        rows_ref.at[pl.ds(pl.multiple_of(group * 8, 8), 8)], spread.at[group], local_sem.at[0]
    )
    own_stay = pltpu.make_async_copy(rows_ref, own, local_sem.at[1])

    own_share.start()
    for t in range(1, 16):
        share(t).start()

    @pl.when(jnp.logical_not(moved))
    def _():
        own_stay.start()

    own_share.wait()
    for t in range(1, 16):
        share_from(t).wait_recv()

    for g in range(16):
        ordered[g] = spread[partner_ref[g]]

    def columns(c):
        step = lax.rem(c + chip, STEPS)
        return pl.ds(pl.multiple_of(step * CHUNK, CHUNK), CHUNK)

    def place(c, dist, member):
        start = SLOT[dist] * 64 + member * 32
        return gathered.at[columns(c), pl.ds(pl.multiple_of(start, 32), 32), :]

    def own_swap(c):
        return pltpu.make_async_remote_copy(
            src_ref=rows_ref.at[columns(c)], dst_ref=own.at[columns(c)],
            send_sem=own_send.at[c], recv_sem=own_recv.at[c],
            device_id=mirror, device_id_type=MESH,
        )

    def share_place(source, member):
        cols = pl.ds(pl.multiple_of(source * 8, 8), 8)
        return gathered.at[cols, pl.ds(pl.multiple_of(member * 32, 32), 32), :]

    def give(t, member):
        to = lax.rem(chip + 8 - t, 8)
        return pltpu.make_async_remote_copy(
            src_ref=ordered.at[to * 2 + member],
            dst_ref=share_place(group, ylo),
            send_sem=part_send.at[t * 2 + member],
            recv_sem=part_recv.at[group],
            device_id={"x": to // 2, "yh": lax.rem(to, 2), "core": ylo, "ylo": member},
            device_id_type=MESH,
        )

    def keep(member):
        return pltpu.make_async_copy(
            ordered.at[chip * 2 + member], share_place(group, ylo), local_sem.at[2]
        )

    def take(c, source_core):
        source = lax.rem(chip + c, 8) * 2 + source_core
        return pltpu.make_async_remote_copy(
            src_ref=ordered.at[0],
            dst_ref=share_place(source, core),
            send_sem=part_send.at[0],
            recv_sem=part_recv.at[source],
            device_id={"core": 1 - core},
            device_id_type=MESH,
        )

    for member in range(2):
        stays = jnp.logical_and(jnp.logical_not(moved), ylo == member)

        @pl.when(stays)
        def _():
            keep(member).start()

        @pl.when(jnp.logical_not(stays))
        def _():
            give(0, member).start()

    for t in range(1, 8):
        for member in range(2):
            give(t, member).start()

    @pl.when(moved)
    def _():
        for c in range(STEPS):
            own_swap(c).start()

    def wait_part(c):
        for source_core in range(2):
            stays = jnp.logical_and(
                c == 0, jnp.logical_and(jnp.logical_not(moved), core == source_core)
            )

            @pl.when(stays)
            def _():
                keep(source_core).wait()

            @pl.when(jnp.logical_not(stays))
            def _():
                take(c, source_core).wait_recv()

    def hop(c, dist, step):
        landed = 4 if dist + step == -4 else dist + step
        return pltpu.make_async_remote_copy(
            src_ref=place(c, dist, core),
            dst_ref=place(c, landed, core),
            send_sem=send_sem.at[c, SLOT[landed] - 1],
            recv_sem=recv_sem.at[c, 0, SLOT[landed]],
            device_id={"z": down if step == 1 else up},
            device_id_type=MESH,
        )

    def across(c, dist):
        return pltpu.make_async_remote_copy(
            src_ref=place(c, dist, core),
            dst_ref=place(c, dist, core),
            send_sem=send_sem.at[c, 7 + SLOT[dist]],
            recv_sem=recv_sem.at[c, 1, SLOT[dist]],
            device_id={"core": 1 - core},
            device_id_type=MESH,
        )

    def across_in(c, dist):
        return pltpu.make_async_remote_copy(
            src_ref=place(c, dist, core),
            dst_ref=place(c, dist, 1 - core),
            send_sem=send_sem.at[c, 7 + SLOT[dist]],
            recv_sem=recv_sem.at[c, 1, SLOT[dist]],
            device_id={"core": 1 - core},
            device_id_type=MESH,
        )

    def result_pieces(tile):
        first, width = TILES[tile]
        for slot in range(first // 64, (first + width) // 64):
            from_z = lax.rem(z + DIST[slot] + 8, 8)
            for member in range(2):
                rows = pl.ds(slot * 64 + member * 32, 32)
                target = pl.ds(pl.multiple_of((member * 8 + from_z) * 32, 32), 32)
                yield slot * 2 + member, result.at[:, rows, :], target

    def result_remote(index, src, target):
        return pltpu.make_async_remote_copy(
            src_ref=src, dst_ref=out_ref.at[:, target, :],
            send_sem=out_send.at[index], recv_sem=out_recv.at[index],
            device_id=mirror, device_id_type=MESH,
        )

    def result_local(index, src, target):
        return pltpu.make_async_copy(src, out_ref.at[:, target, :], out_send.at[index])

    def send_result(tile):
        @pl.when(moved)
        def _():
            for piece in result_pieces(tile):
                result_remote(*piece).start()

        @pl.when(jnp.logical_not(moved))
        def _():
            for piece in result_pieces(tile):
                result_local(*piece).start()

    lane = lax.broadcasted_iota(jnp.int32, (INNER, COLS), 1)
    row = lax.broadcasted_iota(jnp.int32, (INNER, COLS), 0)
    mask = lax.rem(lane // WINDOWS, INNER) == row
    sign = jnp.where(lax.broadcasted_iota(jnp.int32, (CH, COLS), 1) < 64, 1.0, -1.0)

    def load_rows(column):
        value = own[column].astype(jnp.float32)
        x_rows[column] = value
        xs_rows[column] = pltpu.roll(value, 64, 1) * sign

    def cross_column(c, i, lane_slot, tile):
        first, width = TILES[tile]
        column = lax.rem(c + chip, STEPS) * CHUNK + i
        for a in range(CH):
            re_row = jnp.broadcast_to(x_rows[column, pl.ds(a, 1), :], (INNER, COLS))
            im_row = jnp.broadcast_to(xs_rows[column, pl.ds(a, 1), :], (INNER, COLS))
            block = jnp.concatenate(
                [jnp.where(mask, re_row, 0.0), jnp.where(mask, im_row, 0.0)], axis=0
            )
            left[lane_slot, pl.ds(a * 16, 16), :] = block.astype(jnp.bfloat16)
        right = gathered[column, first : first + width, :]
        product = lax.dot_general(
            left[lane_slot], right, (((1,), (1,)), ((), ())), preferred_element_type=jnp.float32
        )
        cross[:, pl.ds(pl.multiple_of(i * 16, 16), 16), :width] = product.astype(
            jnp.bfloat16
        ).reshape(CH, 16, width)

    def lag_channel(c, a, tile):
        first, width = TILES[tile]
        lanes = slice(first, first + width)
        product = jnp.dot(
            lag_ref[lax.rem(c + chip, STEPS)], cross[a, :, :width],
            preferred_element_type=jnp.float32,
        )
        total[a, :, lanes] = jnp.where(c > 0, total[a, :, lanes], 0.0) + product

    def compute(c, tile):
        first, width = TILES[tile]
        lanes = slice(first, first + width)

        @pl.loop(0, CHUNK // GROUP_COLS)
        def _(i):
            for u in range(GROUP_COLS):
                cross_column(c, i * GROUP_COLS + u, u, tile)

        @pl.loop(0, CH // GROUP_CH)
        def _(i):
            for u in range(GROUP_CH):
                lag_channel(c, i * GROUP_CH + u, tile)

        @pl.when(c == STEPS - 1)
        def _():
            @pl.loop(0, CH // 4)
            def _(i):
                for u in range(4):
                    a = i * 4 + u
                    result[a, lanes, :] = total[a, :, lanes].T.astype(jnp.bfloat16)

            send_result(tile)

    def inside(c):
        return jnp.logical_and(c >= 0, c < STEPS)

    @pl.loop(0, 2 * STEPS + 5)
    def _(tick):
        t = tick - 5

        @pl.when(inside(t + 3))
        def _():
            c = t + 3
            hop(c, 0, 1).wait_recv()
            hop(c, 1, 1).start()
            hop(c, 0, -1).wait_recv()
            hop(c, -1, -1).start()
            across(c, 1).start()
            across(c, -1).start()

        @pl.when(inside(t + 5))
        def _():
            c = t + 5
            wait_part(c)
            hop(c, 0, 1).start()
            hop(c, 0, -1).start()
            across(c, 0).start()

        @pl.when(inside(t + 1))
        def _():
            c = t + 1
            hop(c, 1, 1).wait_recv()
            across(c, 2).start()
            hop(c, -1, -1).wait_recv()
            across(c, -2).start()

        @pl.when(inside(t - 1))
        def _():
            c = t - 1
            hop(c, 2, 1).start()
            hop(c, -2, -1).start()

        @pl.when(inside(t - 3))
        def _():
            c = t - 3
            hop(c, 2, 1).wait_recv()
            hop(c, -2, -1).wait_recv()
            across(c, 3).start()
            across(c, -3).start()

        @pl.when(inside(t - 5))
        def _():
            c = t - 5

            @pl.when(lax.rem(c, 2) == 0)
            def _():
                hop(c, 3, 1).start()

            @pl.when(lax.rem(c, 2) == 1)
            def _():
                hop(c, -3, -1).start()

        @pl.when(inside(t - 7))
        def _():
            c = t - 7
            hop(c, 3, 1).wait_recv()
            across(c, 4).start()

        @pl.when(jnp.logical_and(t == 0, jnp.logical_not(moved)))
        def _():
            own_stay.wait()

        @pl.when(inside(t))
        def _():
            @pl.when(moved)
            def _():
                own_swap(t).wait_recv()

            @pl.loop(0, CHUNK // 4)
            def _(i):
                for u in range(4):
                    load_rows(lax.rem(t + chip, STEPS) * CHUNK + i * 4 + u)

            for dist in (0, 1, -1, 2):
                across_in(t, dist).wait_recv()
            compute(t, 0)

        @pl.when(inside(t - 4))
        def _():
            for dist in (-2, 3):
                across_in(t - 4, dist).wait_recv()
            compute(t - 4, 1)

        @pl.when(inside(t - 8))
        def _():
            for dist in (-3, 4):
                across_in(t - 8, dist).wait_recv()
            compute(t - 8, 2)

    for t in range(1, 16):
        share(t).wait_send()

    @pl.when(moved)
    def _():
        for c in range(STEPS):
            own_swap(c).wait_send()

    for member in range(2):
        @pl.when(jnp.logical_or(moved, ylo != member))
        def _():
            give(0, member).wait_send()

    for t in range(1, 8):
        for member in range(2):
            give(t, member).wait_send()

    @pl.loop(0, STEPS)
    def _(c):
        for dist, step in ((0, 1), (0, -1), (1, 1), (-1, -1), (2, 1), (-2, -1), (3, 1)):
            hop(c, dist, step).wait_send()
        for dist in DIST.values():
            across(c, dist).wait_send()

    @pl.when(moved)
    def _():
        for tile in range(len(TILES)):
            for piece in result_pieces(tile):
                result_remote(*piece).wait()

    @pl.when(jnp.logical_not(moved))
    def _():
        for tile in range(len(TILES)):
            for piece in result_pieces(tile):
                result_local(*piece).wait()


def correlate_pairs(partner, rows, table):
    return pl.pallas_call(
        pair_kernel,
        out_shape=jax.ShapeDtypeStruct((CH, 16 * CH, LAGS), jnp.bfloat16),
        in_specs=[
            pl.BlockSpec(memory_space=pltpu.SMEM),
            pl.BlockSpec(memory_space=pl.ANY),
            pl.BlockSpec(memory_space=pltpu.VMEM),
        ],
        out_specs=pl.BlockSpec(memory_space=pl.ANY),
        scratch_shapes=[
            pltpu.VMEM((16, 8, CH, COLS), jnp.bfloat16),
            pltpu.VMEM((16, 8, CH, COLS), jnp.bfloat16),
            pltpu.VMEM((COLS, CH, COLS), jnp.bfloat16),
            pltpu.VMEM((COLS, CH, COLS), jnp.float32),
            pltpu.VMEM((COLS, CH, COLS), jnp.float32),
            pltpu.VMEM((COLS, 16 * CH, COLS), jnp.bfloat16),
            pltpu.VMEM((GROUP_COLS, CH * 16, COLS), jnp.bfloat16),
            pltpu.VMEM((CH, TILE, TILE), jnp.bfloat16),
            pltpu.VMEM((CH, LAGS, 16 * CH), jnp.float32),
            pltpu.VMEM((CH, 16 * CH, LAGS), jnp.bfloat16),
            pltpu.SemaphoreType.DMA((3,)),
            pltpu.SemaphoreType.DMA((16,)),
            pltpu.SemaphoreType.DMA((16,)),
            pltpu.SemaphoreType.DMA((STEPS,)),
            pltpu.SemaphoreType.DMA((STEPS,)),
            pltpu.SemaphoreType.DMA((16,)),
            pltpu.SemaphoreType.DMA((16,)),
            pltpu.SemaphoreType.DMA((STEPS, 2, 8)),
            pltpu.SemaphoreType.DMA((STEPS, 15)),
            pltpu.SemaphoreType.DMA((16,)),
            pltpu.SemaphoreType.DMA((16,)),
        ],
        compiler_params=pltpu.CompilerParams(
            collective_id=0, has_side_effects=True, vmem_limit_bytes=60 << 20
        ),
        name="pairs",
    )(partner, rows, table)


def on_device(spectra, partner):
    whitened = whiten(spectra)
    rows = whitened.reshape(CH, WINDOWS, 2, INNER, COLS)
    rows = jnp.transpose(rows, (4, 0, 2, 3, 1)).reshape(COLS, CH, COLS)
    return correlate_pairs(partner, rows, jnp.asarray(lag_rows()))


def solution(mesh):
    split = Mesh(mesh.devices.reshape(4, 2, 2, 2, 8), AXES)
    return jax.shard_map(
        on_device,
        mesh=split,
        in_specs=(P(AXES, None, None), P()),
        out_specs=P(AXES, None, None),
        check_vma=False,
    )
```

```python
import functools
import math

import jax
import jax.numpy as jnp
import numpy as np
from jax import lax
from jax.experimental import pallas as pl
from jax.experimental.pallas import tpu as pltpu
from jax.sharding import Mesh
from jax.sharding import PartitionSpec as P

LAGS = 128
HALF = 64
FREQS = 1024
WINDOWS = 8
CH = 32
COLS = 128
INNER = 8
CHUNK = 16
STEPS = COLS // CHUNK
TILES = ((0, 256), (256, 128), (384, 128))
TILE = 256
GROUP_COLS = 8
GROUP_CH = 16
AXES = ("x", "yh", "core", "ylo", "z")
MESH = pl.DeviceIdType.MESH

SLOT = {0: 0, 1: 1, -1: 2, 2: 3, -2: 4, 3: 5, -3: 6, 4: 7}
DIST = {slot: dist for dist, slot in SLOT.items()}


def band_matrix():
    positions = jnp.arange(FREQS, dtype=jnp.int32)
    distance = jnp.abs(positions[:, None] - positions[None, :])
    band_ones = (distance <= HALF).astype(jnp.float32)
    counts = (
        jnp.minimum(positions + HALF, FREQS - 1) - jnp.maximum(positions - HALF, 0) + 1
    ).astype(jnp.float32)
    return band_ones, counts


def whiten(spectra):
    real_part = spectra[:, :, :FREQS].astype(jnp.float32)
    imag_part = spectra[:, :, FREQS:].astype(jnp.float32)
    power_sum = jnp.sum(real_part * real_part + imag_part * imag_part, axis=1)
    band_ones, counts = band_matrix()
    smoothed = jnp.dot(power_sum, band_ones, precision=lax.Precision.HIGHEST)
    average = smoothed / (counts * WINDOWS)
    inverse_amp = 1.0 / jnp.sqrt(average + 1e-05)
    factor = jnp.concatenate([inverse_amp, inverse_amp], axis=1)
    return (spectra.astype(jnp.float32) * factor[:, None, :]).astype(jnp.bfloat16)


def lag_rows():
    lag_values = np.arange(LAGS) - LAGS // 2
    columns = np.arange(COLS).reshape(STEPS, CHUNK)
    freq = columns[:, :, None] + COLS * np.arange(INNER)[None, None, :]
    residue = np.mod(freq[:, None, :, :] * lag_values[None, :, None, None], 2 * FREQS)
    angles = np.pi * residue / FREQS
    norm_factor = 1.0 / math.sqrt(WINDOWS * FREQS)
    table = np.stack([np.cos(angles) * norm_factor, -np.sin(angles) * norm_factor], axis=3)
    return table.reshape(STEPS, LAGS, CHUNK * 2 * INNER).astype(jnp.bfloat16)


def pair_kernel(
    partner_ref, rows_ref, lag_ref, out_ref,
    spread, ordered, own, x_rows, xs_rows, gathered, left, cross, total, result,
    local_sem, spread_send, spread_recv, own_send, own_recv, part_send, part_recv,
    recv_sem, send_sem, out_send, out_recv,
):
    x = lax.axis_index("x")
    yh = lax.axis_index("yh")
    core = lax.axis_index("core")
    ylo = lax.axis_index("ylo")
    z = lax.axis_index("z")
    up = lax.rem(z + 1, 8)
    down = lax.rem(z + 7, 8)
    moved = core != ylo
    chip = x * 2 + yh
    group = chip * 2 + core
    mirror = {"core": ylo, "ylo": core}

    barrier = pltpu.get_barrier_semaphore()
    plane = group * 2 + ylo
    for i in range(1, 32):
        other = lax.rem(plane + i, 32)
        where = {
            "x": other // 8, "yh": lax.rem(other // 4, 2),
            "core": lax.rem(other // 2, 2), "ylo": lax.rem(other, 2),
        }
        pl.semaphore_signal(barrier, inc=1, device_id=where, device_id_type=MESH)
    pl.semaphore_signal(barrier, inc=1, device_id={"z": up}, device_id_type=MESH)
    pl.semaphore_signal(barrier, inc=1, device_id={"z": down}, device_id_type=MESH)
    pl.semaphore_wait(barrier, 33)

    def share(t):
        to = lax.rem(group + t, 16)
        return pltpu.make_async_remote_copy(
            src_ref=rows_ref.at[pl.ds(pl.multiple_of(to * 8, 8), 8)],
            dst_ref=spread.at[group],
            send_sem=spread_send.at[t],
            recv_sem=spread_recv.at[group],
            device_id={"x": to // 4, "yh": lax.rem(to // 2, 2), "core": lax.rem(to, 2)},
            device_id_type=MESH,
        )

    def share_from(t):
        source = lax.rem(group + t, 16)
        return pltpu.make_async_remote_copy(
            src_ref=rows_ref.at[pl.ds(0, 8)],
            dst_ref=spread.at[source],
            send_sem=spread_send.at[t],
            recv_sem=spread_recv.at[source],
            device_id={"core": 1 - core},
            device_id_type=MESH,
        )

    own_share = pltpu.make_async_copy(
        rows_ref.at[pl.ds(pl.multiple_of(group * 8, 8), 8)], spread.at[group], local_sem.at[0]
    )
    own_stay = pltpu.make_async_copy(rows_ref, own, local_sem.at[1])

    own_share.start()
    for t in range(1, 16):
        share(t).start()

    @pl.when(jnp.logical_not(moved))
    def _():
        own_stay.start()

    own_share.wait()
    for t in range(1, 16):
        share_from(t).wait_recv()

    for g in range(16):
        ordered[g] = spread[partner_ref[g]]

    def columns(c):
        step = lax.rem(c + chip, STEPS)
        return pl.ds(pl.multiple_of(step * CHUNK, CHUNK), CHUNK)

    def place(c, dist, member):
        start = SLOT[dist] * 64 + member * 32
        return gathered.at[columns(c), pl.ds(pl.multiple_of(start, 32), 32), :]

    def own_swap(c):
        return pltpu.make_async_remote_copy(
            src_ref=rows_ref.at[columns(c)], dst_ref=own.at[columns(c)],
            send_sem=own_send.at[c], recv_sem=own_recv.at[c],
            device_id=mirror, device_id_type=MESH,
        )

    def share_place(source, member):
        cols = pl.ds(pl.multiple_of(source * 8, 8), 8)
        return gathered.at[cols, pl.ds(pl.multiple_of(member * 32, 32), 32), :]

    def give(t, member):
        to = lax.rem(chip + 8 - t, 8)
        return pltpu.make_async_remote_copy(
            src_ref=ordered.at[to * 2 + member],
            dst_ref=share_place(group, ylo),
            send_sem=part_send.at[t * 2 + member],
            recv_sem=part_recv.at[group],
            device_id={"x": to // 2, "yh": lax.rem(to, 2), "core": ylo, "ylo": member},
            device_id_type=MESH,
        )

    def keep(member):
        return pltpu.make_async_copy(
            ordered.at[chip * 2 + member], share_place(group, ylo), local_sem.at[2]
        )

    def take(c, source_core):
        source = lax.rem(chip + c, 8) * 2 + source_core
        return pltpu.make_async_remote_copy(
            src_ref=ordered.at[0],
            dst_ref=share_place(source, core),
            send_sem=part_send.at[0],
            recv_sem=part_recv.at[source],
            device_id={"core": 1 - core},
            device_id_type=MESH,
        )

    for member in range(2):
        stays = jnp.logical_and(jnp.logical_not(moved), ylo == member)

        @pl.when(stays)
        def _():
            keep(member).start()

        @pl.when(jnp.logical_not(stays))
        def _():
            give(0, member).start()

    for t in range(1, 8):
        for member in range(2):
            give(t, member).start()

    @pl.when(moved)
    def _():
        for c in range(STEPS):
            own_swap(c).start()

    def wait_part(c):
        for source_core in range(2):
            stays = jnp.logical_and(
                c == 0, jnp.logical_and(jnp.logical_not(moved), core == source_core)
            )

            @pl.when(stays)
            def _():
                keep(source_core).wait()

            @pl.when(jnp.logical_not(stays))
            def _():
                take(c, source_core).wait_recv()

    def hop(c, dist, step):
        landed = 4 if dist + step == -4 else dist + step
        return pltpu.make_async_remote_copy(
            src_ref=place(c, dist, core),
            dst_ref=place(c, landed, core),
            send_sem=send_sem.at[c, SLOT[landed] - 1],
            recv_sem=recv_sem.at[c, 0, SLOT[landed]],
            device_id={"z": down if step == 1 else up},
            device_id_type=MESH,
        )

    def across(c, dist):
        return pltpu.make_async_remote_copy(
            src_ref=place(c, dist, core),
            dst_ref=place(c, dist, core),
            send_sem=send_sem.at[c, 7 + SLOT[dist]],
            recv_sem=recv_sem.at[c, 1, SLOT[dist]],
            device_id={"core": 1 - core},
            device_id_type=MESH,
        )

    def across_in(c, dist):
        return pltpu.make_async_remote_copy(
            src_ref=place(c, dist, core),
            dst_ref=place(c, dist, 1 - core),
            send_sem=send_sem.at[c, 7 + SLOT[dist]],
            recv_sem=recv_sem.at[c, 1, SLOT[dist]],
            device_id={"core": 1 - core},
            device_id_type=MESH,
        )

    def result_pieces(tile):
        first, width = TILES[tile]
        for slot in range(first // 64, (first + width) // 64):
            from_z = lax.rem(z + DIST[slot] + 8, 8)
            for member in range(2):
                rows = pl.ds(slot * 64 + member * 32, 32)
                target = pl.ds(pl.multiple_of((member * 8 + from_z) * 32, 32), 32)
                yield slot * 2 + member, result.at[:, rows, :], target

    def result_remote(index, src, target):
        return pltpu.make_async_remote_copy(
            src_ref=src, dst_ref=out_ref.at[:, target, :],
            send_sem=out_send.at[index], recv_sem=out_recv.at[index],
            device_id=mirror, device_id_type=MESH,
        )

    def result_local(index, src, target):
        return pltpu.make_async_copy(src, out_ref.at[:, target, :], out_send.at[index])

    def send_result(tile):
        @pl.when(moved)
        def _():
            for piece in result_pieces(tile):
                result_remote(*piece).start()

        @pl.when(jnp.logical_not(moved))
        def _():
            for piece in result_pieces(tile):
                result_local(*piece).start()

    lane = lax.broadcasted_iota(jnp.int32, (INNER, COLS), 1)
    row = lax.broadcasted_iota(jnp.int32, (INNER, COLS), 0)
    mask = lax.rem(lane // WINDOWS, INNER) == row
    sign = jnp.where(lax.broadcasted_iota(jnp.int32, (CH, COLS), 1) < 64, 1.0, -1.0)

    def load_rows(column):
        value = own[column].astype(jnp.float32)
        x_rows[column] = value
        xs_rows[column] = pltpu.roll(value, 64, 1) * sign

    def cross_column(c, i, lane_slot, tile):
        first, width = TILES[tile]
        column = lax.rem(c + chip, STEPS) * CHUNK + i
        for a in range(CH):
            re_row = jnp.broadcast_to(x_rows[column, pl.ds(a, 1), :], (INNER, COLS))
            im_row = jnp.broadcast_to(xs_rows[column, pl.ds(a, 1), :], (INNER, COLS))
            block = jnp.concatenate(
                [jnp.where(mask, re_row, 0.0), jnp.where(mask, im_row, 0.0)], axis=0
            )
            left[lane_slot, pl.ds(a * 16, 16), :] = block.astype(jnp.bfloat16)
        right = gathered[column, first : first + width, :]
        product = lax.dot_general(
            left[lane_slot], right, (((1,), (1,)), ((), ())), preferred_element_type=jnp.float32
        )
        cross[:, pl.ds(pl.multiple_of(i * 16, 16), 16), :width] = product.astype(
            jnp.bfloat16
        ).reshape(CH, 16, width)

    def lag_channel(c, a, tile):
        first, width = TILES[tile]
        lanes = slice(first, first + width)
        product = jnp.dot(
            lag_ref[lax.rem(c + chip, STEPS)], cross[a, :, :width],
            preferred_element_type=jnp.float32,
        )
        total[a, :, lanes] = jnp.where(c > 0, total[a, :, lanes], 0.0) + product

    def compute(c, tile):
        first, width = TILES[tile]
        lanes = slice(first, first + width)

        @pl.loop(0, CHUNK // GROUP_COLS)
        def _(i):
            for u in range(GROUP_COLS):
                cross_column(c, i * GROUP_COLS + u, u, tile)

        @pl.loop(0, CH // GROUP_CH)
        def _(i):
            for u in range(GROUP_CH):
                lag_channel(c, i * GROUP_CH + u, tile)

        @pl.when(c == STEPS - 1)
        def _():
            @pl.loop(0, CH // 4)
            def _(i):
                for u in range(4):
                    a = i * 4 + u
                    result[a, lanes, :] = total[a, :, lanes].T.astype(jnp.bfloat16)

            send_result(tile)

    def inside(c):
        return jnp.logical_and(c >= 0, c < STEPS)

    def start_third(c):
        @pl.when(inside(c))
        def _():
            hop(c, 2, 1).start()
            hop(c, -2, -1).start()

    def end_third(c):
        @pl.when(inside(c))
        def _():
            hop(c, 2, 1).wait_recv()
            across(c, 3).start()
            hop(c, -2, -1).wait_recv()
            across(c, -3).start()

    def middle_tile(c):
        @pl.when(inside(c))
        def _():
            for dist in (-2, 3):
                across_in(c, dist).wait_recv()
            compute(c, 1)

    @pl.loop(0, 18)
    def _(tick):
        t = tick - 3

        @pl.when(inside(t + 3))
        def _():
            c = t + 3
            wait_part(c)
            hop(c, 0, 1).start()
            hop(c, 0, -1).start()
            across(c, 0).start()

        @pl.when(inside(t + 2))
        def _():
            c = t + 2
            hop(c, 0, 1).wait_recv()
            hop(c, 1, 1).start()
            hop(c, 0, -1).wait_recv()
            hop(c, -1, -1).start()
            across(c, 1).start()
            across(c, -1).start()

        @pl.when(inside(t + 1))
        def _():
            c = t + 1
            hop(c, 1, 1).wait_recv()
            across(c, 2).start()
            hop(c, -1, -1).wait_recv()
            across(c, -2).start()

        start_third(2 * t - 11)
        start_third(2 * t - 10)

        @pl.when(inside(2 * t - 18))
        def _():
            hop(2 * t - 18, 3, 1).start()
            hop(2 * t - 17, -3, -1).start()

        end_third(2 * t - 13)
        end_third(2 * t - 12)

        @pl.when(inside(2 * t - 20))
        def _():
            for c in (2 * t - 20, 2 * t - 19):
                hop(c, 3, 1).wait_recv()
                across(c, 4).start()

        @pl.when(jnp.logical_and(t == 0, jnp.logical_not(moved)))
        def _():
            own_stay.wait()

        @pl.when(inside(t))
        def _():
            @pl.when(moved)
            def _():
                own_swap(t).wait_recv()

            @pl.loop(0, CHUNK // 4)
            def _(i):
                for u in range(4):
                    load_rows(lax.rem(t + chip, STEPS) * CHUNK + i * 4 + u)

            for dist in (0, 1, -1, 2):
                across_in(t, dist).wait_recv()
            compute(t, 0)

        @pl.loop(0, 2)
        def _(k):
            middle_tile(2 * t - 15 + k)

        @pl.loop(0, 2)
        def _(k):
            c = 2 * t - 22 + k

            @pl.when(inside(c))
            def _():
                for dist in (-3, 4):
                    across_in(c, dist).wait_recv()
                compute(c, 2)

    for t in range(1, 16):
        share(t).wait_send()

    @pl.when(moved)
    def _():
        for c in range(STEPS):
            own_swap(c).wait_send()

    for member in range(2):
        @pl.when(jnp.logical_or(moved, ylo != member))
        def _():
            give(0, member).wait_send()

    for t in range(1, 8):
        for member in range(2):
            give(t, member).wait_send()

    @pl.loop(0, STEPS)
    def _(c):
        for dist, step in ((0, 1), (0, -1), (1, 1), (-1, -1), (2, 1), (-2, -1), (3, 1)):
            hop(c, dist, step).wait_send()
        for dist in DIST.values():
            across(c, dist).wait_send()

    @pl.when(moved)
    def _():
        for tile in range(len(TILES)):
            for piece in result_pieces(tile):
                result_remote(*piece).wait()

    @pl.when(jnp.logical_not(moved))
    def _():
        for tile in range(len(TILES)):
            for piece in result_pieces(tile):
                result_local(*piece).wait()


def correlate_pairs(partner, rows, table):
    return pl.pallas_call(
        pair_kernel,
        out_shape=jax.ShapeDtypeStruct((CH, 16 * CH, LAGS), jnp.bfloat16),
        in_specs=[
            pl.BlockSpec(memory_space=pltpu.SMEM),
            pl.BlockSpec(memory_space=pl.ANY),
            pl.BlockSpec(memory_space=pltpu.VMEM),
        ],
        out_specs=pl.BlockSpec(memory_space=pl.ANY),
        scratch_shapes=[
            pltpu.VMEM((16, 8, CH, COLS), jnp.bfloat16),
            pltpu.VMEM((16, 8, CH, COLS), jnp.bfloat16),
            pltpu.VMEM((COLS, CH, COLS), jnp.bfloat16),
            pltpu.VMEM((COLS, CH, COLS), jnp.float32),
            pltpu.VMEM((COLS, CH, COLS), jnp.float32),
            pltpu.VMEM((COLS, 16 * CH, COLS), jnp.bfloat16),
            pltpu.VMEM((GROUP_COLS, CH * 16, COLS), jnp.bfloat16),
            pltpu.VMEM((CH, TILE, TILE), jnp.bfloat16),
            pltpu.VMEM((CH, LAGS, 16 * CH), jnp.float32),
            pltpu.VMEM((CH, 16 * CH, LAGS), jnp.bfloat16),
            pltpu.SemaphoreType.DMA((3,)),
            pltpu.SemaphoreType.DMA((16,)),
            pltpu.SemaphoreType.DMA((16,)),
            pltpu.SemaphoreType.DMA((STEPS,)),
            pltpu.SemaphoreType.DMA((STEPS,)),
            pltpu.SemaphoreType.DMA((16,)),
            pltpu.SemaphoreType.DMA((16,)),
            pltpu.SemaphoreType.DMA((STEPS, 2, 8)),
            pltpu.SemaphoreType.DMA((STEPS, 15)),
            pltpu.SemaphoreType.DMA((16,)),
            pltpu.SemaphoreType.DMA((16,)),
        ],
        compiler_params=pltpu.CompilerParams(
            collective_id=0, has_side_effects=True, vmem_limit_bytes=60 << 20
        ),
        name="pairs",
    )(partner, rows, table)


def on_device(spectra, partner):
    whitened = whiten(spectra)
    rows = whitened.reshape(CH, WINDOWS, 2, INNER, COLS)
    rows = jnp.transpose(rows, (4, 0, 2, 3, 1)).reshape(COLS, CH, COLS)
    return correlate_pairs(partner, rows, jnp.asarray(lag_rows()))


def solution(mesh):
    split = Mesh(mesh.devices.reshape(4, 2, 2, 2, 8), AXES)
    return jax.shard_map(
        on_device,
        mesh=split,
        in_specs=(P(AXES, None, None), P()),
        out_specs=P(AXES, None, None),
        check_vma=False,
    )
```

```python
import functools
import math

import jax
import jax.numpy as jnp
import numpy as np
from jax import lax
from jax.experimental import pallas as pl
from jax.experimental.pallas import tpu as pltpu
from jax.sharding import Mesh
from jax.sharding import PartitionSpec as P

LAGS = 128
HALF = 64
FREQS = 1024
WINDOWS = 8
CH = 32
COLS = 128
INNER = 8
CHUNK = 16
STEPS = COLS // CHUNK
TILES = ((0, 256), (256, 128), (384, 128))
TILE = 256
GROUP_COLS = 8
GROUP_CH = 16
AXES = ("x", "yh", "core", "ylo", "z")
MESH = pl.DeviceIdType.MESH

SLOT = {0: 0, 1: 1, -1: 2, 2: 3, -2: 4, 3: 5, -3: 6, 4: 7}
DIST = {slot: dist for dist, slot in SLOT.items()}


def band_matrix():
    positions = jnp.arange(FREQS, dtype=jnp.int32)
    distance = jnp.abs(positions[:, None] - positions[None, :])
    band_ones = (distance <= HALF).astype(jnp.float32)
    counts = (
        jnp.minimum(positions + HALF, FREQS - 1) - jnp.maximum(positions - HALF, 0) + 1
    ).astype(jnp.float32)
    return band_ones, counts


def whiten(spectra):
    real_part = spectra[:, :, :FREQS].astype(jnp.float32)
    imag_part = spectra[:, :, FREQS:].astype(jnp.float32)
    power_sum = jnp.sum(real_part * real_part + imag_part * imag_part, axis=1)
    band_ones, counts = band_matrix()
    smoothed = jnp.dot(power_sum, band_ones, precision=lax.Precision.HIGHEST)
    average = smoothed / (counts * WINDOWS)
    inverse_amp = 1.0 / jnp.sqrt(average + 1e-05)
    factor = jnp.concatenate([inverse_amp, inverse_amp], axis=1)
    return (spectra.astype(jnp.float32) * factor[:, None, :]).astype(jnp.bfloat16)


def lag_rows():
    lag_values = np.arange(LAGS) - LAGS // 2
    columns = np.arange(COLS).reshape(STEPS, CHUNK)
    freq = columns[:, :, None] + COLS * np.arange(INNER)[None, None, :]
    residue = np.mod(freq[:, None, :, :] * lag_values[None, :, None, None], 2 * FREQS)
    angles = np.pi * residue / FREQS
    norm_factor = 1.0 / math.sqrt(WINDOWS * FREQS)
    table = np.stack([np.cos(angles) * norm_factor, -np.sin(angles) * norm_factor], axis=3)
    return table.reshape(STEPS, LAGS, CHUNK * 2 * INNER).astype(jnp.bfloat16)


def pair_kernel(
    partner_ref, rows_ref, lag_ref, out_ref,
    spread, ordered, own, x_rows, xs_rows, gathered, left, left_pair, cross, total, result,
    local_sem, spread_send, spread_recv, own_send, own_recv, part_send, part_recv,
    recv_sem, send_sem, out_send, out_recv,
):
    x = lax.axis_index("x")
    yh = lax.axis_index("yh")
    core = lax.axis_index("core")
    ylo = lax.axis_index("ylo")
    z = lax.axis_index("z")
    up = lax.rem(z + 1, 8)
    down = lax.rem(z + 7, 8)
    moved = core != ylo
    chip = x * 2 + yh
    group = chip * 2 + core
    mirror = {"core": ylo, "ylo": core}

    barrier = pltpu.get_barrier_semaphore()
    plane = group * 2 + ylo
    for i in range(1, 32):
        other = lax.rem(plane + i, 32)
        where = {
            "x": other // 8, "yh": lax.rem(other // 4, 2),
            "core": lax.rem(other // 2, 2), "ylo": lax.rem(other, 2),
        }
        pl.semaphore_signal(barrier, inc=1, device_id=where, device_id_type=MESH)
    pl.semaphore_signal(barrier, inc=1, device_id={"z": up}, device_id_type=MESH)
    pl.semaphore_signal(barrier, inc=1, device_id={"z": down}, device_id_type=MESH)
    pl.semaphore_wait(barrier, 33)

    def share(t):
        to = lax.rem(group + t, 16)
        return pltpu.make_async_remote_copy(
            src_ref=rows_ref.at[pl.ds(pl.multiple_of(to * 8, 8), 8)],
            dst_ref=spread.at[group],
            send_sem=spread_send.at[t],
            recv_sem=spread_recv.at[group],
            device_id={"x": to // 4, "yh": lax.rem(to // 2, 2), "core": lax.rem(to, 2)},
            device_id_type=MESH,
        )

    def share_from(t):
        source = lax.rem(group + t, 16)
        return pltpu.make_async_remote_copy(
            src_ref=rows_ref.at[pl.ds(0, 8)],
            dst_ref=spread.at[source],
            send_sem=spread_send.at[t],
            recv_sem=spread_recv.at[source],
            device_id={"core": 1 - core},
            device_id_type=MESH,
        )

    own_share = pltpu.make_async_copy(
        rows_ref.at[pl.ds(pl.multiple_of(group * 8, 8), 8)], spread.at[group], local_sem.at[0]
    )
    own_stay = pltpu.make_async_copy(rows_ref, own, local_sem.at[1])

    own_share.start()
    for t in range(1, 16):
        share(t).start()

    @pl.when(jnp.logical_not(moved))
    def _():
        own_stay.start()

    own_share.wait()
    for t in range(1, 16):
        share_from(t).wait_recv()

    for g in range(16):
        ordered[g] = spread[partner_ref[g]]

    def columns(c):
        step = lax.rem(c + chip, STEPS)
        return pl.ds(pl.multiple_of(step * CHUNK, CHUNK), CHUNK)

    def place(c, dist, member):
        start = SLOT[dist] * 64 + member * 32
        return gathered.at[columns(c), pl.ds(pl.multiple_of(start, 32), 32), :]

    def own_swap(c):
        return pltpu.make_async_remote_copy(
            src_ref=rows_ref.at[columns(c)], dst_ref=own.at[columns(c)],
            send_sem=own_send.at[c], recv_sem=own_recv.at[c],
            device_id=mirror, device_id_type=MESH,
        )

    def share_place(source, member):
        cols = pl.ds(pl.multiple_of(source * 8, 8), 8)
        return gathered.at[cols, pl.ds(pl.multiple_of(member * 32, 32), 32), :]

    def give(t, member):
        to = lax.rem(chip + 8 - t, 8)
        return pltpu.make_async_remote_copy(
            src_ref=ordered.at[to * 2 + member],
            dst_ref=share_place(group, ylo),
            send_sem=part_send.at[t * 2 + member],
            recv_sem=part_recv.at[group],
            device_id={"x": to // 2, "yh": lax.rem(to, 2), "core": ylo, "ylo": member},
            device_id_type=MESH,
        )

    def keep(member):
        return pltpu.make_async_copy(
            ordered.at[chip * 2 + member], share_place(group, ylo), local_sem.at[2]
        )

    def take(c, source_core):
        source = lax.rem(chip + c, 8) * 2 + source_core
        return pltpu.make_async_remote_copy(
            src_ref=ordered.at[0],
            dst_ref=share_place(source, core),
            send_sem=part_send.at[0],
            recv_sem=part_recv.at[source],
            device_id={"core": 1 - core},
            device_id_type=MESH,
        )

    for member in range(2):
        stays = jnp.logical_and(jnp.logical_not(moved), ylo == member)

        @pl.when(stays)
        def _():
            keep(member).start()

        @pl.when(jnp.logical_not(stays))
        def _():
            give(0, member).start()

    for t in range(1, 8):
        for member in range(2):
            give(t, member).start()

    @pl.when(moved)
    def _():
        for c in range(STEPS):
            own_swap(c).start()

    def wait_part(c):
        for source_core in range(2):
            stays = jnp.logical_and(
                c == 0, jnp.logical_and(jnp.logical_not(moved), core == source_core)
            )

            @pl.when(stays)
            def _():
                keep(source_core).wait()

            @pl.when(jnp.logical_not(stays))
            def _():
                take(c, source_core).wait_recv()

    def hop(c, dist, step):
        landed = 4 if dist + step == -4 else dist + step
        return pltpu.make_async_remote_copy(
            src_ref=place(c, dist, core),
            dst_ref=place(c, landed, core),
            send_sem=send_sem.at[c, SLOT[landed] - 1],
            recv_sem=recv_sem.at[c, 0, SLOT[landed]],
            device_id={"z": down if step == 1 else up},
            device_id_type=MESH,
        )

    def across(c, dist):
        return pltpu.make_async_remote_copy(
            src_ref=place(c, dist, core),
            dst_ref=place(c, dist, core),
            send_sem=send_sem.at[c, 7 + SLOT[dist]],
            recv_sem=recv_sem.at[c, 1, SLOT[dist]],
            device_id={"core": 1 - core},
            device_id_type=MESH,
        )

    def across_in(c, dist):
        return pltpu.make_async_remote_copy(
            src_ref=place(c, dist, core),
            dst_ref=place(c, dist, 1 - core),
            send_sem=send_sem.at[c, 7 + SLOT[dist]],
            recv_sem=recv_sem.at[c, 1, SLOT[dist]],
            device_id={"core": 1 - core},
            device_id_type=MESH,
        )

    def result_pieces(tile):
        first, width = TILES[tile]
        for slot in range(first // 64, (first + width) // 64):
            from_z = lax.rem(z + DIST[slot] + 8, 8)
            for member in range(2):
                rows = pl.ds(slot * 64 + member * 32, 32)
                target = pl.ds(pl.multiple_of((member * 8 + from_z) * 32, 32), 32)
                yield slot * 2 + member, result.at[:, rows, :], target

    def result_remote(index, src, target):
        return pltpu.make_async_remote_copy(
            src_ref=src, dst_ref=out_ref.at[:, target, :],
            send_sem=out_send.at[index], recv_sem=out_recv.at[index],
            device_id=mirror, device_id_type=MESH,
        )

    def result_local(index, src, target):
        return pltpu.make_async_copy(src, out_ref.at[:, target, :], out_send.at[index])

    def send_result(tile):
        @pl.when(moved)
        def _():
            for piece in result_pieces(tile):
                result_remote(*piece).start()

        @pl.when(jnp.logical_not(moved))
        def _():
            for piece in result_pieces(tile):
                result_local(*piece).start()

    lane = lax.broadcasted_iota(jnp.int32, (INNER, COLS), 1)
    row = lax.broadcasted_iota(jnp.int32, (INNER, COLS), 0)
    mask = lax.rem(lane // WINDOWS, INNER) == row
    sign = jnp.where(lax.broadcasted_iota(jnp.int32, (CH, COLS), 1) < 64, 1.0, -1.0)

    def load_rows(column):
        value = own[column].astype(jnp.float32)
        x_rows[column] = value
        xs_rows[column] = pltpu.roll(value, 64, 1) * sign

    def cross_column(c, i, lane_slot, tile):
        first, width = TILES[tile]
        column = lax.rem(c + chip, STEPS) * CHUNK + i
        for a in range(CH):
            re_row = jnp.broadcast_to(x_rows[column, pl.ds(a, 1), :], (INNER, COLS))
            im_row = jnp.broadcast_to(xs_rows[column, pl.ds(a, 1), :], (INNER, COLS))
            block = jnp.concatenate(
                [jnp.where(mask, re_row, 0.0), jnp.where(mask, im_row, 0.0)], axis=0
            )
            left[lane_slot, pl.ds(a * 16, 16), :] = block.astype(jnp.bfloat16)
        right = gathered[column, first : first + width, :]
        product = lax.dot_general(
            left[lane_slot], right, (((1,), (1,)), ((), ())), preferred_element_type=jnp.float32
        )
        cross[:, pl.ds(pl.multiple_of(i * 16, 16), 16), :width] = product.astype(
            jnp.bfloat16
        ).reshape(CH, 16, width)

    def cross_pair(c, i, pair_slot, tile):
        first, width = TILES[tile]
        column = lax.rem(c + chip, STEPS) * CHUNK + i
        for half in range(2):
            for a in range(CH):
                re_row = jnp.broadcast_to(x_rows[column + half, pl.ds(a, 1), :], (INNER, COLS))
                im_row = jnp.broadcast_to(xs_rows[column + half, pl.ds(a, 1), :], (INNER, COLS))
                block = jnp.concatenate(
                    [jnp.where(mask, re_row, 0.0), jnp.where(mask, im_row, 0.0)], axis=0
                )
                left_pair[
                    pair_slot, pl.ds(a * 16, 16), half * COLS : (half + 1) * COLS
                ] = block.astype(jnp.bfloat16)
        none = jnp.zeros((width, COLS), jnp.bfloat16)
        right = jnp.concatenate(
            [
                jnp.concatenate([gathered[column, first : first + width, :], none], axis=1),
                jnp.concatenate([none, gathered[column + 1, first : first + width, :]], axis=1),
            ],
            axis=0,
        )
        product = lax.dot_general(
            left_pair[pair_slot], right, (((1,), (1,)), ((), ())),
            preferred_element_type=jnp.float32,
        )
        product = product.astype(jnp.bfloat16).reshape(CH // 2, 2, 16, 2 * width)
        for half in range(2):
            rows = pl.ds(pl.multiple_of((i + half) * 16, 16), 16)
            lanes = slice(half * width, (half + 1) * width)
            for odd in range(2):
                cross[: CH // 2, rows, odd * width : (odd + 1) * width] = product[:, odd, :, lanes]

    def lag_pair(c, pair, tile):
        first, width = TILES[tile]
        lanes = slice(first, first + width)
        product = jnp.dot(
            lag_ref[lax.rem(c + chip, STEPS)], cross[pair], preferred_element_type=jnp.float32
        )
        for odd in range(2):
            a = pair * 2 + odd
            total[a, :, lanes] = (
                jnp.where(c > 0, total[a, :, lanes], 0.0)
                + product[:, odd * width : (odd + 1) * width]
            )

    def lag_channel(c, a, tile):
        first, width = TILES[tile]
        lanes = slice(first, first + width)
        product = jnp.dot(
            lag_ref[lax.rem(c + chip, STEPS)], cross[a, :, :width],
            preferred_element_type=jnp.float32,
        )
        total[a, :, lanes] = jnp.where(c > 0, total[a, :, lanes], 0.0) + product

    def compute(c, tile):
        first, width = TILES[tile]
        lanes = slice(first, first + width)

        if width == TILE:

            @pl.loop(0, CHUNK // GROUP_COLS)
            def _(i):
                for u in range(GROUP_COLS):
                    cross_column(c, i * GROUP_COLS + u, u, tile)

            @pl.loop(0, CH // GROUP_CH)
            def _(i):
                for u in range(GROUP_CH):
                    lag_channel(c, i * GROUP_CH + u, tile)

        else:

            @pl.loop(0, CHUNK // GROUP_COLS)
            def _(i):
                for u in range(GROUP_COLS // 2):
                    cross_pair(c, i * GROUP_COLS + u * 2, u, tile)

            for pair in range(CH // 2):
                lag_pair(c, pair, tile)

        @pl.when(c == STEPS - 1)
        def _():
            @pl.loop(0, CH // 4)
            def _(i):
                for u in range(4):
                    a = i * 4 + u
                    result[a, lanes, :] = total[a, :, lanes].T.astype(jnp.bfloat16)

            send_result(tile)

    def inside(c):
        return jnp.logical_and(c >= 0, c < STEPS)

    def start_third(c):
        @pl.when(inside(c))
        def _():
            hop(c, 2, 1).start()
            hop(c, -2, -1).start()

    def end_third(c):
        @pl.when(inside(c))
        def _():
            hop(c, 2, 1).wait_recv()
            across(c, 3).start()
            hop(c, -2, -1).wait_recv()
            across(c, -3).start()

    def middle_tile(c):
        @pl.when(inside(c))
        def _():
            for dist in (-2, 3):
                across_in(c, dist).wait_recv()
            compute(c, 1)

    @pl.loop(0, 18)
    def _(tick):
        t = tick - 3

        @pl.when(inside(t + 3))
        def _():
            c = t + 3
            wait_part(c)
            hop(c, 0, 1).start()
            hop(c, 0, -1).start()
            across(c, 0).start()

        @pl.when(inside(t + 2))
        def _():
            c = t + 2
            hop(c, 0, 1).wait_recv()
            hop(c, 1, 1).start()
            hop(c, 0, -1).wait_recv()
            hop(c, -1, -1).start()
            across(c, 1).start()
            across(c, -1).start()

        @pl.when(inside(t + 1))
        def _():
            c = t + 1
            hop(c, 1, 1).wait_recv()
            across(c, 2).start()
            hop(c, -1, -1).wait_recv()
            across(c, -2).start()

        start_third(2 * t - 11)
        start_third(2 * t - 10)

        @pl.when(inside(2 * t - 18))
        def _():
            hop(2 * t - 18, 3, 1).start()
            hop(2 * t - 17, -3, -1).start()

        end_third(2 * t - 13)
        end_third(2 * t - 12)

        @pl.when(inside(2 * t - 20))
        def _():
            for c in (2 * t - 20, 2 * t - 19):
                hop(c, 3, 1).wait_recv()
                across(c, 4).start()

        @pl.when(jnp.logical_and(t == 0, jnp.logical_not(moved)))
        def _():
            own_stay.wait()

        @pl.when(inside(t))
        def _():
            @pl.when(moved)
            def _():
                own_swap(t).wait_recv()

            @pl.loop(0, CHUNK // 4)
            def _(i):
                for u in range(4):
                    load_rows(lax.rem(t + chip, STEPS) * CHUNK + i * 4 + u)

            for dist in (0, 1, -1, 2):
                across_in(t, dist).wait_recv()
            compute(t, 0)

        @pl.loop(0, 2)
        def _(k):
            middle_tile(2 * t - 15 + k)

        @pl.loop(0, 2)
        def _(k):
            c = 2 * t - 22 + k

            @pl.when(inside(c))
            def _():
                for dist in (-3, 4):
                    across_in(c, dist).wait_recv()
                compute(c, 2)

    for t in range(1, 16):
        share(t).wait_send()

    @pl.when(moved)
    def _():
        for c in range(STEPS):
            own_swap(c).wait_send()

    for member in range(2):
        @pl.when(jnp.logical_or(moved, ylo != member))
        def _():
            give(0, member).wait_send()

    for t in range(1, 8):
        for member in range(2):
            give(t, member).wait_send()

    @pl.loop(0, STEPS)
    def _(c):
        for dist, step in ((0, 1), (0, -1), (1, 1), (-1, -1), (2, 1), (-2, -1), (3, 1)):
            hop(c, dist, step).wait_send()
        for dist in DIST.values():
            across(c, dist).wait_send()

    @pl.when(moved)
    def _():
        for tile in range(len(TILES)):
            for piece in result_pieces(tile):
                result_remote(*piece).wait()

    @pl.when(jnp.logical_not(moved))
    def _():
        for tile in range(len(TILES)):
            for piece in result_pieces(tile):
                result_local(*piece).wait()


def correlate_pairs(partner, rows, table):
    return pl.pallas_call(
        pair_kernel,
        out_shape=jax.ShapeDtypeStruct((CH, 16 * CH, LAGS), jnp.bfloat16),
        in_specs=[
            pl.BlockSpec(memory_space=pltpu.SMEM),
            pl.BlockSpec(memory_space=pl.ANY),
            pl.BlockSpec(memory_space=pltpu.VMEM),
        ],
        out_specs=pl.BlockSpec(memory_space=pl.ANY),
        scratch_shapes=[
            pltpu.VMEM((16, 8, CH, COLS), jnp.bfloat16),
            pltpu.VMEM((16, 8, CH, COLS), jnp.bfloat16),
            pltpu.VMEM((COLS, CH, COLS), jnp.bfloat16),
            pltpu.VMEM((COLS, CH, COLS), jnp.float32),
            pltpu.VMEM((COLS, CH, COLS), jnp.float32),
            pltpu.VMEM((COLS, 16 * CH, COLS), jnp.bfloat16),
            pltpu.VMEM((GROUP_COLS, CH * 16, COLS), jnp.bfloat16),
            pltpu.VMEM((GROUP_COLS // 2, CH * 16, 2 * COLS), jnp.bfloat16),
            pltpu.VMEM((CH, TILE, TILE), jnp.bfloat16),
            pltpu.VMEM((CH, LAGS, 16 * CH), jnp.float32),
            pltpu.VMEM((CH, 16 * CH, LAGS), jnp.bfloat16),
            pltpu.SemaphoreType.DMA((3,)),
            pltpu.SemaphoreType.DMA((16,)),
            pltpu.SemaphoreType.DMA((16,)),
            pltpu.SemaphoreType.DMA((STEPS,)),
            pltpu.SemaphoreType.DMA((STEPS,)),
            pltpu.SemaphoreType.DMA((16,)),
            pltpu.SemaphoreType.DMA((16,)),
            pltpu.SemaphoreType.DMA((STEPS, 2, 8)),
            pltpu.SemaphoreType.DMA((STEPS, 15)),
            pltpu.SemaphoreType.DMA((16,)),
            pltpu.SemaphoreType.DMA((16,)),
        ],
        compiler_params=pltpu.CompilerParams(
            collective_id=0, has_side_effects=True, vmem_limit_bytes=60 << 20
        ),
        name="pairs",
    )(partner, rows, table)


def on_device(spectra, partner):
    whitened = whiten(spectra)
    rows = whitened.reshape(CH, WINDOWS, 2, INNER, COLS)
    rows = jnp.transpose(rows, (4, 0, 2, 3, 1)).reshape(COLS, CH, COLS)
    return correlate_pairs(partner, rows, jnp.asarray(lag_rows()))


def solution(mesh):
    split = Mesh(mesh.devices.reshape(4, 2, 2, 2, 8), AXES)
    return jax.shard_map(
        on_device,
        mesh=split,
        in_specs=(P(AXES, None, None), P()),
        out_specs=P(AXES, None, None),
        check_vma=False,
    )
```
